32 devices in a mesh: groups: 1, gx: 32 (over z, y, x, core).
Axes of the slice: x: 2, y: 2, z: 4, core: 2. Of those that a mesh axis runs over, the one named last changes fastest.
Arguments:
- features: bfloat16 [32, 32, 32768], P(None, ('groups', 'gx')), may hold values from -6 to 6
- block_scale: float32 [32, 32], P(None, ('groups', 'gx')), may hold values from 0.25 to 4
- spec_weight: bfloat16 [2, 32, 32, 8192], P(None, None, None, 'gx'), may hold values from -12 to 12
- bypass_weight: bfloat16 [32, 32], replicated, may hold values from -1 to 1
- mlp_in: bfloat16 [128, 32], replicated, may hold values from -1 to 1
- mlp_out: bfloat16 [32, 128], replicated, may hold values from -0.5 to 0.5
- decode_weight: bfloat16 [2, 32], replicated, may hold values from -1 to 1
- zone_ids: int32 [32, 32768], P(('groups', 'gx')), may hold values from 0 to 7
- face_open: int32 [3, 32, 32768], P(None, ('groups', 'gx')), may hold values 0 or 1
- perm_table: float32 [8], replicated, may hold values from 0.05 to 20
Outputs:
- fields: float32 [2, 32, 32768], P(None, ('groups', 'gx'))
- residual: float32 [32, 32768], P(('groups', 'gx'))
The draws below stay inside these ranges and needn't reach their ends.
All inputs are finite; a program needn't handle non-finite values. No bound on the sum of `face_open` on one device may be relied on, other than what follows from the above.
Results may differ from the reference program's by a relative error of at most 0.011.
Values sent between devices are 32-bit elements; how exact they have to be, the bound alone decides.
A program may use at most 64 MiB of HBM per device.

```python
import math
import jax
import jax.numpy as jnp
from jax import lax

W = 32
HID = 128
NY = 512
NZ = 64
KX = 32
KY = 32
KZ = 8
ZONES = 8
NX = 32
NYZ = 32768
MODES = 8192


def with_ends(values, key, smallest, high):
    index_at = [jax.random.randint(jax.random.fold_in(key, axis), (), 0, length) for axis, length in enumerate(values.shape)]
    widest = values.shape.index(max(values.shape))
    neighbour = index_at[:widest] + [(index_at[widest] + 1) % values.shape[widest]] + index_at[widest + 1:]
    return values.at[tuple(index_at)].set(smallest).at[tuple(neighbour)].set(high)


def steps_of(rng, dims, split, smallest, largest):
    gain, own = 1.0, jax.random.fold_in(rng, 6)
    for axis_at, shards_of in split:
        heights = jnp.exp(jax.random.uniform(jax.random.fold_in(own, axis_at), (shards_of,), jnp.float32, smallest / len(split), largest / len(split)))
        gain = gain * jnp.repeat(heights, dims[axis_at] // shards_of).reshape([-1 if axis == axis_at else 1 for axis in range(len(dims))])
    return gain


def normal_values(key, shape, scale, limit, cuts=(), kind=jnp.bfloat16):
    level = steps_of(key, shape, cuts, -0.22, 0.18) if cuts else 1.0
    array = jax.random.normal(key, shape, jnp.float32) * scale * level
    return jnp.minimum(jnp.maximum(array, -limit), limit).astype(kind)


def setup_inputs(seed: int = 0, part: int = 0) -> dict:
    streams_of = jax.random.split(jax.random.key(seed), 11)
    own_keys = jax.random.split(jax.random.fold_in(streams_of[10], part), 11)
    features = normal_values(own_keys[0], (W, NX, NYZ), 1.0, 6.0, ((1, 32),))
    block_scale = jnp.clip(jnp.exp(math.log(4.0) - 2.7725887 * jax.random.uniform(own_keys[1], (W, NX), jnp.float32) ** steps_of(own_keys[1], (W, NX), ((1, 32),), -0.2, 0.2)), 0.25, 4.0)
    spec_weight = normal_values(streams_of[2], (2, W, W, MODES), 2.0, 12.0, ((3, 32),))
    bypass_weight = normal_values(streams_of[3], (W, W), W ** -0.5, 1.0)
    mlp_in = normal_values(streams_of[4], (HID, W), W ** -0.5, 1.0)
    mlp_out = normal_values(streams_of[5], (W, HID), HID ** -0.5, 0.5)
    decode_weight = normal_values(streams_of[6], (2, W), W ** -0.5, 1.0)
    zone_ids = with_ends(jax.random.randint(own_keys[7], (NX, NYZ), 0, ZONES), jax.random.fold_in(own_keys[7], 1), 0, ZONES - 1).astype(jnp.int32)
    face_open = with_ends((jax.random.randint(own_keys[8], (3, NX, NYZ), 0, 5) < 4).astype(jnp.int32), jax.random.fold_in(own_keys[8], 1), 0, 1)
    perm_table = jnp.clip(jnp.exp(jax.random.uniform(streams_of[9], (ZONES,), jnp.float32, math.log(0.05), math.log(20.0))), 0.05, 20.0)
    return dict(features=features, block_scale=block_scale, spec_weight=spec_weight, bypass_weight=bypass_weight, mlp_in=mlp_in, mlp_out=mlp_out, decode_weight=decode_weight, zone_ids=zone_ids, face_open=face_open, perm_table=perm_table)


def mode_index(count, length):
    half = count // 2
    return jnp.concatenate([jnp.arange(half), jnp.arange(length - half, length)]).astype(jnp.int32)


def lookup(zone_ids, perm_table):
    total = jnp.zeros(zone_ids.shape, jnp.float32)
    for zone in range(ZONES):
        total = total + jnp.where(zone_ids == zone, perm_table[zone], 0.0)
    return total


def face_flux(pressure, mobility, perm, opened, next_pressure, next_mobility, next_perm):
    harmonic = 2.0 * perm * next_perm / (perm + next_perm)
    return opened * harmonic * 0.5 * (mobility + next_mobility) * (pressure - next_pressure)


def ahead(field, axis):
    count = field.shape[axis]
    upper = lax.slice_in_dim(field, 1, count, axis=axis)
    return jnp.concatenate([upper, jnp.zeros_like(lax.slice_in_dim(field, 0, 1, axis=axis))], axis=axis)


def behind(field, axis):
    count = field.shape[axis]
    lower = lax.slice_in_dim(field, 0, count - 1, axis=axis)
    return jnp.concatenate([jnp.zeros_like(lax.slice_in_dim(field, 0, 1, axis=axis)), lower], axis=axis)


def reference(features, block_scale, spec_weight, bypass_weight, mlp_in, mlp_out, decode_weight, zone_ids, face_open, perm_table):
    highest = lax.Precision.HIGHEST
    values = (features.astype(jnp.float32) * block_scale[:, :, None]).astype(jnp.bfloat16)
    grid = values.astype(jnp.float32).reshape(W, NX, NY, NZ)
    index_x = mode_index(KX, NX)
    index_y = mode_index(KY, NY)

    def forward_channel(channel):
        spectrum = jnp.fft.rfftn(channel, axes=(0, 1, 2))
        block = jnp.transpose(spectrum[index_x][:, index_y][:, :, :KZ], (1, 2, 0))
        return jnp.real(block).reshape(-1), jnp.imag(block).reshape(-1)

    modes_real, modes_imag = lax.map(forward_channel, grid)
    mix = spec_weight.astype(jnp.float32)
    out_real = jnp.einsum('im,iom->om', modes_real, mix[0], precision=highest) - jnp.einsum('im,iom->om', modes_imag, mix[1], precision=highest)
    out_imag = jnp.einsum('im,iom->om', modes_real, mix[1], precision=highest) + jnp.einsum('im,iom->om', modes_imag, mix[0], precision=highest)

    def inverse_channel(pair):
        block = jnp.transpose((pair[0] + 1j * pair[1]).reshape(KY, KZ, KX), (2, 0, 1))
        full = jnp.zeros((NX, NY, NZ // 2 + 1), block.dtype)
        full = full.at[index_x[:, None], index_y[None, :], :KZ].set(block)
        return jnp.fft.irfftn(full, s=(NX, NY, NZ), axes=(0, 1, 2)).astype(jnp.float32)

    spectral = lax.map(inverse_channel, (out_real, out_imag)).reshape(W, NX, NY * NZ)

    def plane(pair):
        spec_row, value_row = pair
        pre = spec_row + jnp.dot(bypass_weight, value_row, preferred_element_type=jnp.float32)
        lifted = jax.nn.gelu(pre).astype(jnp.bfloat16)
        hidden = jax.nn.gelu(jnp.dot(mlp_in, lifted, preferred_element_type=jnp.float32)).astype(jnp.bfloat16)
        mixed_out = jnp.dot(mlp_out, hidden, preferred_element_type=jnp.float32).astype(jnp.bfloat16)
        return jnp.dot(decode_weight, mixed_out, preferred_element_type=jnp.float32)

    decoded = lax.map(plane, (jnp.transpose(spectral, (1, 0, 2)), jnp.transpose(values, (1, 0, 2))))
    pressure = decoded[:, 0]
    saturation = jax.nn.sigmoid(decoded[:, 1])
    fields = jnp.stack([pressure, saturation])
    mobility = saturation * saturation / (saturation * saturation + 0.5 * (1.0 - saturation) * (1.0 - saturation))
    perm = lookup(zone_ids, perm_table)
    shape3 = (NX, NY, NZ)
    pressure3 = pressure.reshape(shape3)
    mobility3 = mobility.reshape(shape3)
    perm3 = perm.reshape(shape3)
    opened = face_open.astype(jnp.float32).reshape(3, NX, NY, NZ)
    residual = jnp.zeros(shape3, jnp.float32)
    for axis in range(3):
        flux = face_flux(pressure3, mobility3, perm3, opened[axis], ahead(pressure3, axis), ahead(mobility3, axis), ahead(perm3, axis))
        residual = residual + (flux - behind(flux, axis))
    return fields, residual.reshape(NX, NY * NZ)
```

```python
import math

import jax
import jax.numpy as jnp
import numpy as np
from jax import lax
from jax.experimental import pallas as pl
from jax.experimental.pallas import tpu as pltpu
from jax.sharding import PartitionSpec as P

NY = 512
NZ = 64
KX = 32
KY = 32
KZ = 8
ZONES = 8
YC = 16
LANES = 128
KYZ = KY * KZ
CHUNK = YC * NZ
CHUNKS = NY // YC
GROUP = 8
F32 = jnp.float32
BF16 = jnp.bfloat16
VMEM = pl.BlockSpec(memory_space=pltpu.VMEM)


def signed(count):
    steps = np.arange(count)
    return np.where(steps < count // 2, steps, steps - count)


def pair(table):
    high = table.astype(BF16)
    low = (table - high.astype(np.float64)).astype(BF16)
    return jnp.asarray(high), jnp.asarray(low)


def plane_table():
    ky = np.repeat(signed(KY), KZ)[:, None]
    kz = np.tile(np.arange(KZ), KY)[:, None]
    yy = np.repeat(np.arange(YC), NZ)[None]
    zz = np.tile(np.arange(NZ), YC)[None]
    angle = 2.0 * math.pi * ((ky * yy / NY + kz * zz / NZ) % 1.0)
    return pair(np.concatenate([np.cos(angle), -np.sin(angle)]))


def chunk_turns():
    ky = np.repeat(signed(KY), KZ)[None]
    angle = 2.0 * math.pi * ((ky * (YC * np.arange(CHUNKS))[:, None] / NY) % 1.0)
    return jnp.asarray(np.stack([np.cos(angle), np.sin(angle)]).astype(np.float32))


def line_table(total_x, lines):
    angle = 2.0 * math.pi * ((signed(KX)[None] * np.arange(total_x)[:, None] / total_x) % 1.0)
    same = np.eye(lines)
    parts = [
        np.einsum("xk,lm->xlmk", part, same).reshape(total_x * lines, lines * KX)
        for part in (np.cos(angle), np.sin(angle))
    ]
    return pair(np.concatenate(parts, axis=1))


def gelu(x):
    return 0.5 * x * (1.0 + jnp.tanh(x * (0.7978845608028654 + 0.035677408136300125 * (x * x))))


def matmul(a, b, dims):
    return lax.dot_general(a, b, ((dims[:1], dims[1:]), ((), ())), preferred_element_type=F32)


def column(row):
    count = row.shape[1]
    shape = (count, count)
    same = lax.broadcasted_iota(jnp.int32, shape, 0) == lax.broadcasted_iota(jnp.int32, shape, 1)
    return jnp.sum(jnp.where(same, row, 0.0), axis=1, keepdims=True)


def scaled(cells, scale):
    return (cells.astype(F32) * scale).astype(BF16)


def split(x):
    high = x.astype(BF16)
    return high, (x - high.astype(F32)).astype(BF16)


def fine(a, table, dims):
    high, low = split(a)
    return (
        matmul(high, table[0], dims) + matmul(low, table[0], dims) + matmul(high, table[1], dims)
    )


def forward(f_ref, scale, high_ref, low_ref, turn_ref, held, ready):
    width = f_ref.shape[0]
    real = jnp.zeros((width, KYZ), F32)
    imag = jnp.zeros((width, KYZ), F32)
    for first in range(0, CHUNKS, GROUP):
        ready(first // GROUP)
        for j in range(first, first + GROUP):
            held[j * width : (j + 1) * width, :] = scaled(
                f_ref[:, j * CHUNK : (j + 1) * CHUNK], scale
            )
        some = held[first * width : (first + GROUP) * width, :]
        part = matmul(some, high_ref[...], (1, 1)) + matmul(some, low_ref[...], (1, 1))
        for j in range(first, first + GROUP):
            rows = part[(j - first) * width : (j - first + 1) * width]
            re, im = rows[:, :KYZ], rows[:, KYZ:]
            c, s = turn_ref[0, j : j + 1, :], turn_ref[1, j : j + 1, :]
            real = real + re * c + im * s
            imag = imag + im * c - re * s
    return jnp.concatenate([real, imag], axis=0).T


def exchange(n, me, src, dst, send_sem, recv_sem, meanwhile=None):
    def copy(d):
        peer = lax.rem(me + d, n)
        return pltpu.make_async_remote_copy(
            src_ref=src.at[peer],
            dst_ref=dst.at[me],
            send_sem=send_sem.at[d],
            recv_sem=recv_sem.at[d],
            device_id={"gx": peer},
            device_id_type=pl.DeviceIdType.MESH,
        )

    def start(d, carry):
        copy(d).start()
        return carry

    def finish(d, carry):
        copy(d).wait()
        return carry

    lax.fori_loop(1, n, start, 0)
    dst[me] = src[me]
    if meanwhile is not None:
        meanwhile()
    lax.fori_loop(1, n, finish, 0)


def one_hot(rows, cols, on_row, on_col):
    row = on_row(lax.broadcasted_iota(jnp.int32, (rows, cols), 0))
    col = on_col(lax.broadcasted_iota(jnp.int32, (rows, cols), 1))
    return jnp.where(row == col, 1.0, 0.0)


def block_diagonal(weight, rows, cols):
    tall = matmul(
        one_hot(GROUP * rows, rows, lambda r: r % rows, lambda c: c).astype(BF16), weight, (1, 0)
    ).astype(BF16)
    full = matmul(
        tall, one_hot(cols, GROUP * cols, lambda r: r, lambda c: c % cols).astype(BF16), (1, 0)
    )
    mask = one_hot(GROUP * rows, GROUP * cols, lambda r: r // rows, lambda c: c // cols)
    return (full * mask).astype(BF16)


def mode_kernel(
    n, norm, f_hbm, scale_hbm, high_hbm, low_hbm, turn_hbm, line_hbm, line_low_hbm, w_hbm,
    bypass_hbm, in_hbm, outw_hbm, dec_hbm, zone_hbm, open_hbm, perm_hbm, fields_ref, out_ref,
    f_ref, scale_ref, high_ref, low_ref, turn_ref, line_ref, line_low, w_ref,
    bypass_ref, in_ref, outw_ref, dec_ref, zone_ref, open_ref, perm_ref,
    held, turned, folded, wide_in, wide_by, up, down, zone_up, zone_down, open_down, send, recv,
    a_ref, lines, modes, back, landed, load_sem, send_a, recv_a, send_b, recv_b,
):
    me = lax.axis_index("gx")
    barrier = pltpu.get_barrier_semaphore()

    def greet(d, carry):
        pl.semaphore_signal(
            barrier, inc=1, device_id={"gx": lax.rem(me + d, n)},
            device_id_type=pl.DeviceIdType.MESH,
        )
        return carry

    lax.fori_loop(1, n, greet, 0)
    groups = CHUNKS // GROUP
    span = GROUP * CHUNK
    pieces = [
        (f_hbm.at[:, g * span : (g + 1) * span], f_ref.at[:, g * span : (g + 1) * span])
        for g in range(groups)
    ]
    wanted = [(high_hbm, high_ref), (low_hbm, low_ref), (scale_hbm, scale_ref), (turn_hbm, turn_ref)]
    wanted += pieces + [(line_hbm, line_ref), (line_low_hbm, line_low), (w_hbm, w_ref)]
    wanted += [(bypass_hbm, bypass_ref), (in_hbm, in_ref), (outw_hbm, outw_ref)]
    wanted += [(dec_hbm, dec_ref), (zone_hbm, zone_ref), (open_hbm, open_ref)]
    wanted += [(perm_hbm, perm_ref)]
    loads = [
        pltpu.make_async_copy(src, dst, load_sem.at[k]) for k, (src, dst) in enumerate(wanted)
    ]
    for load in loads:
        load.start()
    for load in loads[:4]:
        load.wait()
    scale = column(scale_ref[...])
    seen = forward(
        f_ref, scale, high_ref, low_ref, turn_ref, held, lambda g: loads[4 + g].wait()
    )
    a_ref[...] = seen.reshape(a_ref.shape)
    pl.semaphore_wait(barrier, n - 1)

    def weights():
        for load in loads[4 + groups :]:
            load.wait()
        width, hid = in_ref.shape
        fold = jnp.dot(dec_ref[...], outw_ref[...], preferred_element_type=F32)
        high = fold.astype(BF16).astype(F32)
        low = fold - high
        row = lax.broadcasted_iota(jnp.int32, (GROUP, hid), 0)
        for r in range(GROUP):
            rows = [
                jnp.where(row == r, part[k : k + 1, :], 0.0)
                for k in range(2)
                for part in (high, low)
            ]
            folded[:, r * hid : (r + 1) * hid] = jnp.concatenate(rows, axis=0).astype(BF16)
        wide_by[...] = block_diagonal(bypass_ref[...], width, width)
        wide_in[...] = block_diagonal(in_ref[...].T, hid, width)

    exchange(n, me, a_ref, lines, send_a, recv_a, weights)
    count, per, both = lines.shape
    width = both // 2
    own = line_ref.shape[1] // 2
    spread = fine(
        lines[...].reshape(count * per, both), (line_ref[...], line_low[...]), (0, 0)
    )
    modes[:width] = spread[:width, :own] + spread[width:, own:]
    modes[width:] = spread[width:, :own] - spread[:width, own:]

    def mix(i, carry):
        real, imag = carry
        re, im = modes[pl.ds(i, 1), :], modes[pl.ds(width + i, 1), :]
        wr, wi = w_ref[0, i].astype(F32), w_ref[1, i].astype(F32)
        return real + (re * wr - im * wi), imag + (re * wi + im * wr)

    zero = jnp.zeros((width, own), F32)
    real, imag = lax.fori_loop(0, width, mix, (zero, zero), unroll=4)
    line = me * per + lax.broadcasted_iota(jnp.int32, (1, own), 1) // KX
    weight = jnp.where(line % KZ == 0, norm, 2.0 * norm)
    real, imag = real * weight, imag * weight
    spun = jnp.concatenate(
        [jnp.concatenate([real, -imag], axis=1), jnp.concatenate([imag, real], axis=1)], axis=0
    )
    high, low = split(spun)
    turned_back = (
        matmul(line_ref[...], high, (1, 1))
        + matmul(line_ref[...], low, (1, 1))
        + matmul(line_low[...], high, (1, 1))
    )
    back[...] = turned_back.reshape(back.shape)
    has_up, has_down = me < n - 1, me > 0

    def copy(src, dst, at, peer):
        return pltpu.make_async_remote_copy(
            src_ref=src, dst_ref=dst, send_sem=send.at[at], recv_sem=recv.at[at],
            device_id={"gx": peer}, device_id_type=pl.DeviceIdType.MESH,
        )

    tall = GROUP * CHUNK // LANES
    base = 2 + groups

    def part(ref, g):
        return ref.at[:, pl.ds(pl.multiple_of(g * tall, tall), tall)]

    def up_copy(g):
        return copy(part(fields_ref, g), part(down, g), 2 + g, me + 1)

    def down_copy(g):
        return copy(part(fields_ref, g), part(up, g), base + 1 + g, me - 1)

    to_up = [copy(zone_ref, zone_down, 0, me + 1), copy(open_ref.at[0], open_down, 1, me + 1)]
    to_down = [copy(zone_ref, zone_up, base, me - 1)]

    def outer():
        @pl.when(has_up)
        def _():
            to_up[0].start()
            to_up[1].start()

        @pl.when(has_down)
        def _():
            to_down[0].start()

    exchange(n, me, back, landed, send_b, recv_b, outer)
    both = landed[...].reshape(KYZ, 2 * width).T
    re, im = both[:width], both[width:]
    for j in range(CHUNKS):
        c, s = turn_ref[0, j : j + 1, :], turn_ref[1, j : j + 1, :]
        turned[j * width : (j + 1) * width, :KYZ] = (re * c - im * s).astype(BF16)
        turned[j * width : (j + 1) * width, KYZ:] = (im * c + re * s).astype(BF16)
    tile = 2 * LANES

    def group(g, carry):
        rows = pl.ds(pl.multiple_of(g * GROUP * width, GROUP * width), GROUP * width)
        for at in range(0, CHUNK, tile):
            pre = matmul(turned[rows, :], high_ref[:, at : at + tile], (1, 0)) + matmul(
                wide_by[...], held[rows, at : at + tile], (1, 0)
            )
            lifted = gelu(pre).astype(BF16)
            hidden = gelu(matmul(wide_in[...], lifted, (1, 0))).astype(BF16)
            decoded = matmul(folded[...], hidden, (1, 0))
            pressure = decoded[:GROUP] + decoded[GROUP : 2 * GROUP]
            saturation = jax.nn.sigmoid(decoded[2 * GROUP : 3 * GROUP] + decoded[3 * GROUP :])
            for k in range(tile // LANES):
                where = pl.ds(g * tall + at // LANES + k, GROUP, stride=CHUNK // LANES)
                lanes = slice(k * LANES, (k + 1) * LANES)
                fields_ref[0, where, :] = pressure[:, lanes]
                fields_ref[1, where, :] = saturation[:, lanes]

        @pl.when(has_up)
        def _():
            up_copy(g).start()

        @pl.when(has_down)
        def _():
            down_copy(g).start()

        return carry

    lax.fori_loop(0, groups, group, 0)

    def lookup(zones):
        total = jnp.zeros(zones.shape, F32)
        for zone in range(ZONES):
            total = jnp.where(zones == zone, perm_ref[zone], total)
        return total

    def triple(fields, zones):
        return fields[0], mobility_of(fields[1]), lookup(zones[...])

    here = triple(fields_ref, zone_ref)
    shape = here[0].shape
    last = shape[0] - 1
    lane = lax.broadcasted_iota(jnp.int32, shape, 1)
    line = lax.broadcasted_iota(jnp.int32, shape, 0)
    opened = [open_ref[d].astype(F32) for d in range(3)]

    def ahead_y(x):
        a = pltpu.roll(x, NZ, 1)
        return jnp.where(lane < NZ, a, pltpu.roll(a, last, 0))

    def behind_y(x):
        a = pltpu.roll(x, NZ, 1)
        return jnp.where(lane < NZ, pltpu.roll(a, 1, 0), a)

    flux = flux_of(opened[1], here, [ahead_y(x) for x in here], (line < last) | (lane < NZ))
    total = flux - behind_y(flux)
    flux = flux_of(
        opened[2], here, [pltpu.roll(x, LANES - 1, 1) for x in here], lane % NZ < NZ - 1
    )
    out_ref[...] = total + (flux - pltpu.roll(flux, 1, 1))

    @pl.when(has_up)
    def _():
        for c in to_up + [up_copy(g) for g in range(groups)]:
            c.wait_send()
        for at, dst in enumerate([zone_up] + [part(up, g) for g in range(groups)]):
            copy(dst, dst, base + at, me + 1).wait_recv()
        there = triple(up, zone_up)
        out_ref[...] += flux_of(open_ref[0].astype(F32), triple(fields_ref, zone_ref), there, True)

    @pl.when(has_down)
    def _():
        for c in to_down + [down_copy(g) for g in range(groups)]:
            c.wait_send()
        for at, dst in enumerate([zone_down, open_down] + [part(down, g) for g in range(groups)]):
            copy(dst, dst, at, me - 1).wait_recv()
        there = triple(down, zone_down)
        out_ref[...] -= flux_of(
            open_down[...].astype(F32), there, triple(fields_ref, zone_ref), True
        )


def mobility_of(s):
    return s * s / (s * s + 0.5 * (1.0 - s) * (1.0 - s))


def flux_of(opened, here, there, inside):
    p, m, k = here
    pn, mn, kn = there
    flux = opened * (2.0 * k * kn / (k + kn)) * 0.5 * (m + mn) * (p - pn)
    return jnp.where(inside, flux, 0.0)


def deliver_kernel(fields_ref, residual_ref, fields_out, residual_out, gone):
    stores = [
        pltpu.make_async_copy(src, dst, gone.at[k])
        for k, (src, dst) in enumerate([(fields_ref, fields_out), (residual_ref, residual_out)])
    ]
    for store in stores:
        store.start()
    for store in stores:
        store.wait()


def body(
    features,
    block_scale,
    spec_weight,
    bypass_weight,
    mlp_in,
    mlp_out,
    decode_weight,
    zone_ids,
    face_open,
    perm_table,
):
    width, rows, cells = features.shape
    n = lax.axis_size("gx")
    per = KYZ // n
    own = per * KX
    tall = cells // LANES
    zones = zone_ids.reshape(tall, LANES)
    opened = face_open.reshape(3, tall, LANES)
    flat = features.reshape(width, cells)
    table, turns, line = plane_table(), chunk_turns(), line_table(rows * n, per)
    hid = mlp_in.shape[0]
    shape = (n, per, 2 * width)
    block = pltpu.VMEM(shape, F32)
    sems = pltpu.SemaphoreType.DMA((n,))
    norm = 1.0 / (rows * n * NY * NZ)
    sources = (
        flat, block_scale.T, *table, turns, *line, spec_weight,
        bypass_weight, mlp_in.T, mlp_out, decode_weight, zones, opened,
    )
    plane = pltpu.VMEM((tall, LANES), jnp.int32)
    near = pltpu.VMEM((2, tall, LANES), F32)
    groups = CHUNKS // GROUP
    links = pltpu.SemaphoreType.DMA((3 + 2 * groups,))
    fields, residual = pl.pallas_call(
        lambda *refs: mode_kernel(n, norm, *refs),
        out_shape=(
            pltpu.VMEM((2, tall, LANES), F32),
            pltpu.VMEM((tall, LANES), F32),
        ),
        in_specs=[pl.BlockSpec(memory_space=pltpu.HBM)] * (len(sources) + 1),
        out_specs=(VMEM, VMEM),
        scratch_shapes=[pltpu.VMEM(source.shape, source.dtype) for source in sources]
        + [
            pltpu.SMEM(perm_table.shape, F32),
            pltpu.VMEM((CHUNKS * width, CHUNK), BF16),
            pltpu.VMEM((CHUNKS * width, 2 * KYZ), BF16),
            pltpu.VMEM((4 * GROUP, GROUP * hid), BF16),
            pltpu.VMEM((GROUP * hid, GROUP * width), BF16),
            pltpu.VMEM((GROUP * width, GROUP * width), BF16),
            near,
            near,
            plane,
            plane,
            plane,
            links,
            links,
            block,
            block,
            pltpu.VMEM((2 * width, own), F32),
            block,
            block,
            pltpu.SemaphoreType.DMA((len(sources) + groups,)),
            sems,
            sems,
            sems,
            sems,
        ],
        compiler_params=pltpu.CompilerParams(
            vmem_limit_bytes=60 << 20, collective_id=0, has_side_effects=True
        ),
        name="layer",
    )(*(pltpu.with_memory_space_constraint(x, pltpu.HBM) for x in (*sources, perm_table)))
    anywhere = pl.BlockSpec(memory_space=pl.ANY)
    fields, residual = pl.pallas_call(
        deliver_kernel,
        out_shape=(
            jax.ShapeDtypeStruct((2, tall, LANES), F32),
            jax.ShapeDtypeStruct((tall, LANES), F32),
        ),
        in_specs=[VMEM, VMEM],
        out_specs=(anywhere, anywhere),
        scratch_shapes=[pltpu.SemaphoreType.DMA((2,))],
        name="deliver",
    )(*(pltpu.with_memory_space_constraint(x, pltpu.VMEM) for x in (fields, residual)))
    return fields.reshape(2, rows, cells), residual.reshape(rows, cells)


def solution(mesh):
    in_specs = (
        P(None, ("groups", "gx"), None),
        P(None, ("groups", "gx")),
        P(None, None, None, "gx"),
        P(),
        P(),
        P(),
        P(),
        P(("groups", "gx"), None),
        P(None, ("groups", "gx"), None),
        P(),
    )
    out_specs = (P(None, ("groups", "gx"), None), P(("groups", "gx"), None))
    return jax.shard_map(body, mesh=mesh, in_specs=in_specs, out_specs=out_specs, check_vma=False)
```

```python
import math

import jax
import jax.numpy as jnp
import numpy as np
from jax import lax
from jax.experimental import pallas as pl
from jax.experimental.pallas import tpu as pltpu
from jax.sharding import PartitionSpec as P

NY = 512
NZ = 64
KX = 32
KY = 32
KZ = 8
ZONES = 8
YC = 16
LANES = 128
KYZ = KY * KZ
HALF = KYZ // 2
CHUNK = YC * NZ
CHUNKS = NY // YC
GROUP = 8
F32 = jnp.float32
BF16 = jnp.bfloat16
VMEM = pl.BlockSpec(memory_space=pltpu.VMEM)


def signed(count):
    steps = np.arange(count)
    return np.where(steps < count // 2, steps, steps - count)


def pair(table):
    high = table.astype(BF16)
    low = (table - high.astype(np.float64)).astype(BF16)
    return jnp.asarray(high), jnp.asarray(low)


def ordered_ky():
    return np.concatenate([signed(KY)[::2], signed(KY)[1::2]])


def plane_table():
    ky = np.repeat(ordered_ky(), KZ)[:, None]
    kz = np.tile(np.arange(KZ), KY)[:, None]
    yy = np.repeat(np.arange(YC), NZ)[None]
    zz = np.tile(np.arange(NZ), YC)[None]
    angle = 2.0 * math.pi * ((ky * yy / NY + kz * zz / NZ) % 1.0)
    parts = [part[at : at + HALF] for at in (0, HALF) for part in (np.cos(angle), -np.sin(angle))]
    return jnp.asarray(np.concatenate(parts).astype(BF16))


def chunk_turns():
    ky = np.repeat(ordered_ky(), KZ)[None]
    angle = 2.0 * math.pi * ((ky * (YC * np.arange(CHUNKS))[:, None] / NY) % 1.0)
    return jnp.asarray(np.stack([np.cos(angle), np.sin(angle)]).astype(np.float32))


def line_table(total_x, lines):
    angle = 2.0 * math.pi * ((signed(KX)[None] * np.arange(total_x)[:, None] / total_x) % 1.0)
    same = np.eye(lines)
    parts = [
        np.einsum("xk,lm->xlmk", part, same).reshape(total_x * lines, lines * KX)
        for part in (np.cos(angle), np.sin(angle))
    ]
    return pair(np.concatenate(parts, axis=1))


def gelu_twice(x):
    x = x.astype(BF16)
    return x + x * jnp.tanh(x * (BF16(0.7978845608028654) + BF16(0.035677408136300125) * (x * x)))


def matmul(a, b, dims):
    return lax.dot_general(a, b, ((dims[:1], dims[1:]), ((), ())), preferred_element_type=F32)


def column(row):
    count = row.shape[1]
    shape = (count, count)
    same = lax.broadcasted_iota(jnp.int32, shape, 0) == lax.broadcasted_iota(jnp.int32, shape, 1)
    return jnp.sum(jnp.where(same, row, 0.0), axis=1, keepdims=True)


def scaled(cells, scale):
    return (cells.astype(F32) * scale).astype(BF16)


def split(x):
    high = x.astype(BF16)
    return high, (x - high.astype(F32)).astype(BF16)


def fine(a, table, dims):
    high, low = split(a)
    return (
        matmul(high, table[0], dims) + matmul(low, table[0], dims) + matmul(high, table[1], dims)
    )


def forward(f_ref, scale, table_ref, turn_ref, held, ready):
    width = f_ref.shape[0]
    real = [jnp.zeros((width, HALF), F32)] * 2
    imag = [jnp.zeros((width, HALF), F32)] * 2
    for first in range(0, CHUNKS, GROUP):
        ready(first // GROUP)
        for j in range(first, first + GROUP):
            held[j * width : (j + 1) * width, :] = scaled(
                f_ref[:, j * CHUNK : (j + 1) * CHUNK], scale
            )
        part = matmul(held[first * width : (first + GROUP) * width, :], table_ref[...], (1, 1))
        for j in range(first, first + GROUP):
            rows = part[(j - first) * width : (j - first + 1) * width]
            for h in range(2):
                at = h * HALF
                re, im = rows[:, 2 * at : 2 * at + HALF], rows[:, 2 * at + HALF : 2 * at + KYZ]
                c, s = (turn_ref[k, j : j + 1, at : at + HALF] for k in range(2))
                real[h] = real[h] + re * c + im * s
                imag[h] = imag[h] + im * c - re * s
    both = [jnp.concatenate(x, axis=1) for x in (real, imag)]
    return jnp.concatenate(both, axis=0).T


def slot(device, n):
    share = KZ * n // KYZ
    ky = device // share
    return (ky % 2 * (KY // 2) + ky // 2) * share + device % share


def exchange(n, me, src, dst, place, spot, send_sem, recv_sem, meanwhile=None):
    def copy(d):
        peer = lax.rem(me + d, n)
        return pltpu.make_async_remote_copy(
            src_ref=src.at[place(peer)],
            dst_ref=dst.at[spot(me)],
            send_sem=send_sem.at[d],
            recv_sem=recv_sem.at[d],
            device_id={"gx": peer},
            device_id_type=pl.DeviceIdType.MESH,
        )

    def start(d, carry):
        copy(d).start()
        return carry

    def finish(d, carry):
        copy(d).wait()
        return carry

    lax.fori_loop(1, n, start, 0)
    dst[spot(me)] = src[place(me)]
    if meanwhile is not None:
        meanwhile()
    lax.fori_loop(1, n, finish, 0)


def one_hot(rows, cols, on_row, on_col):
    row = on_row(lax.broadcasted_iota(jnp.int32, (rows, cols), 0))
    col = on_col(lax.broadcasted_iota(jnp.int32, (rows, cols), 1))
    return jnp.where(row == col, 1.0, 0.0)


def block_diagonal(weight, rows, cols):
    tall = matmul(
        one_hot(GROUP * rows, rows, lambda r: r % rows, lambda c: c).astype(BF16), weight, (1, 0)
    ).astype(BF16)
    full = matmul(
        tall, one_hot(cols, GROUP * cols, lambda r: r, lambda c: c % cols).astype(BF16), (1, 0)
    )
    mask = one_hot(GROUP * rows, GROUP * cols, lambda r: r // rows, lambda c: c // cols)
    return (full * mask).astype(BF16)


def mode_kernel(
    n, norm, f_hbm, scale_hbm, table_hbm, turn_hbm, line_hbm, line_low_hbm, w_hbm,
    bypass_hbm, in_hbm, outw_hbm, dec_hbm, zone_hbm, open_hbm, perm_hbm, fields_ref, out_ref,
    f_ref, scale_ref, table_ref, turn_ref, line_ref, line_low, w_ref,
    bypass_ref, in_ref, outw_ref, dec_ref, zone_ref, open_ref, perm_ref,
    held, turned, lifted, hidden, skip, folded, wide_in, wide_by, up, down, zone_up, zone_down, open_down, send, recv,
    a_ref, lines, modes, back, landed, load_sem, send_a, recv_a, send_b, recv_b,
):
    me = lax.axis_index("gx")
    barrier = pltpu.get_barrier_semaphore()

    def greet(d, carry):
        pl.semaphore_signal(
            barrier, inc=1, device_id={"gx": lax.rem(me + d, n)},
            device_id_type=pl.DeviceIdType.MESH,
        )
        return carry

    lax.fori_loop(1, n, greet, 0)
    groups = CHUNKS // GROUP
    span = GROUP * CHUNK
    pieces = [
        (f_hbm.at[:, g * span : (g + 1) * span], f_ref.at[:, g * span : (g + 1) * span])
        for g in range(groups)
    ]
    wanted = [(table_hbm, table_ref), (scale_hbm, scale_ref), (turn_hbm, turn_ref)]
    wanted += pieces + [(line_hbm, line_ref), (line_low_hbm, line_low), (w_hbm, w_ref)]
    wanted += [(bypass_hbm, bypass_ref), (in_hbm, in_ref), (outw_hbm, outw_ref)]
    wanted += [(dec_hbm, dec_ref), (zone_hbm, zone_ref), (open_hbm, open_ref)]
    wanted += [(perm_hbm, perm_ref)]
    loads = [
        pltpu.make_async_copy(src, dst, load_sem.at[k]) for k, (src, dst) in enumerate(wanted)
    ]
    for load in loads:
        load.start()
    for load in loads[:3]:
        load.wait()
    scale = column(scale_ref[...])
    seen = forward(
        f_ref, scale, table_ref, turn_ref, held, lambda g: loads[3 + g].wait()
    )
    a_ref[...] = seen.reshape(a_ref.shape)
    pl.semaphore_wait(barrier, n - 1)

    def weights():
        for load in loads[3 + groups :]:
            load.wait()
        width, hid = in_ref.shape
        fold = jnp.dot(dec_ref[...], outw_ref[...], preferred_element_type=F32) * 0.5
        high = fold.astype(BF16).astype(F32)
        low = fold - high
        row = lax.broadcasted_iota(jnp.int32, (GROUP, hid), 0)
        for r in range(GROUP):
            rows = [
                jnp.where(row == r, part[k : k + 1, :], 0.0)
                for k in range(2)
                for part in (high, low)
            ]
            folded[:, r * hid : (r + 1) * hid] = jnp.concatenate(rows, axis=0).astype(BF16)
        wide_by[...] = block_diagonal(bypass_ref[...], width, width)
        wide_in[...] = block_diagonal(in_ref[...].T, hid, width) * BF16(0.5)
        tall_rows = GROUP * width

        def bypass(g, carry):
            rows = pl.ds(pl.multiple_of(g * tall_rows, tall_rows), tall_rows)
            skip[rows, :] = matmul(wide_by[...], held[rows, :], (1, 0))
            return carry

        lax.fori_loop(0, groups, bypass, 0)

    exchange(n, me, a_ref, lines, lambda d: slot(d, n), lambda d: d, send_a, recv_a, weights)
    count, per, both = lines.shape
    width = both // 2
    own = line_ref.shape[1] // 2
    spread = fine(
        lines[...].reshape(count * per, both), (line_ref[...], line_low[...]), (0, 0)
    )
    modes[:width] = spread[:width, :own] + spread[width:, own:]
    modes[width:] = spread[width:, :own] - spread[:width, own:]

    def mix(i, carry):
        real, imag = carry
        re, im = modes[pl.ds(i, 1), :], modes[pl.ds(width + i, 1), :]
        wr, wi = w_ref[0, i].astype(F32), w_ref[1, i].astype(F32)
        return real + (re * wr - im * wi), imag + (re * wi + im * wr)

    zero = jnp.zeros((width, own), F32)
    real, imag = lax.fori_loop(0, width, mix, (zero, zero), unroll=4)
    line = me * per + lax.broadcasted_iota(jnp.int32, (1, own), 1) // KX
    weight = jnp.where(line % KZ == 0, norm, 2.0 * norm)
    real, imag = real * weight, imag * weight
    spun = jnp.concatenate(
        [jnp.concatenate([real, -imag], axis=1), jnp.concatenate([imag, real], axis=1)], axis=0
    )
    high, low = split(spun)
    turned_back = (
        matmul(line_ref[...], high, (1, 1))
        + matmul(line_ref[...], low, (1, 1))
        + matmul(line_low[...], high, (1, 1))
    )
    back[...] = turned_back.reshape(back.shape)
    has_up, has_down = me < n - 1, me > 0

    def copy(src, dst, at, peer):
        return pltpu.make_async_remote_copy(
            src_ref=src, dst_ref=dst, send_sem=send.at[at], recv_sem=recv.at[at],
            device_id={"gx": peer}, device_id_type=pl.DeviceIdType.MESH,
        )

    tall = GROUP * CHUNK // LANES
    base = 2 + groups

    def part(ref, g):
        return ref.at[:, pl.ds(pl.multiple_of(g * tall, tall), tall)]

    def up_copy(g):
        return copy(part(fields_ref, g), part(down, g), 2 + g, me + 1)

    def down_copy(g):
        return copy(part(fields_ref, g), part(up, g), base + 1 + g, me - 1)

    to_up = [copy(zone_ref, zone_down, 0, me + 1), copy(open_ref.at[0], open_down, 1, me + 1)]
    to_down = [copy(zone_ref, zone_up, base, me - 1)]

    def outer():
        @pl.when(has_up)
        def _():
            to_up[0].start()
            to_up[1].start()

        @pl.when(has_down)
        def _():
            to_down[0].start()

    exchange(n, me, back, landed, lambda d: d, lambda d: slot(d, n), send_b, recv_b, outer)
    both = landed[...].reshape(KYZ, 2 * width).T
    re, im = both[:width], both[width:]
    for j in range(CHUNKS // 2):
        c, s = turn_ref[0, j : j + 1, :], turn_ref[1, j : j + 1, :]
        spun_re, spun_im = (re * c - im * s).astype(BF16), (im * c + re * s).astype(BF16)
        for h in range(2):
            at = h * HALF
            rows = slice(j * width, (j + 1) * width)
            turned[rows, 2 * at : 2 * at + HALF] = spun_re[:, at : at + HALF]
            turned[rows, 2 * at + HALF : 2 * at + KYZ] = spun_im[:, at : at + HALF]
    tile = 2 * LANES
    hid = in_ref.shape[1]
    tall_rows, tall_hid, pairs = GROUP * width, GROUP * hid, groups // 2
    for g in range(pairs):
        low = slice(g * tall_rows, (g + 1) * tall_rows)
        high = slice((g + pairs) * tall_rows, (g + pairs + 1) * tall_rows)
        for at in range(0, CHUNK, tile):
            cols = slice(at, at + tile)
            even = matmul(turned[low, :KYZ], table_ref[:KYZ, cols], (1, 0))
            odd = matmul(turned[low, KYZ:], table_ref[KYZ:, cols], (1, 0))
            lifted[:tall_rows, cols] = gelu_twice(even + odd + skip[low, cols])
            lifted[tall_rows:, cols] = gelu_twice(even - odd + skip[high, cols])
        for k in range(2):
            at_g = g + k * pairs
            for at in range(0, CHUNK, tile):
                cols = slice(at, at + tile)
                hidden[k * tall_hid : (k + 1) * tall_hid, cols] = gelu_twice(
                    matmul(wide_in[...], lifted[k * tall_rows : (k + 1) * tall_rows, cols], (1, 0))
                )
            decoded = matmul(folded[...], hidden[k * tall_hid : (k + 1) * tall_hid, :], (1, 0))
            pressure = decoded[:GROUP] + decoded[GROUP : 2 * GROUP]
            saturation = jax.nn.sigmoid(decoded[2 * GROUP : 3 * GROUP] + decoded[3 * GROUP :])
            for r in range(CHUNK // LANES):
                where = pl.ds(at_g * tall + r, GROUP, stride=CHUNK // LANES)
                lanes = slice(r * LANES, (r + 1) * LANES)
                fields_ref[0, where, :] = pressure[:, lanes]
                fields_ref[1, where, :] = saturation[:, lanes]

            @pl.when(has_up)
            def _(at_g=at_g):
                up_copy(at_g).start()

            @pl.when(has_down)
            def _(at_g=at_g):
                down_copy(at_g).start()

    def lookup(zones):
        total = jnp.zeros(zones.shape, F32)
        for zone in range(ZONES):
            total = jnp.where(zones == zone, perm_ref[zone], total)
        return total

    def triple(fields, zones):
        return fields[0], mobility_of(fields[1]), lookup(zones[...])

    here = triple(fields_ref, zone_ref)
    shape = here[0].shape
    last = shape[0] - 1
    lane = lax.broadcasted_iota(jnp.int32, shape, 1)
    line = lax.broadcasted_iota(jnp.int32, shape, 0)
    opened = [open_ref[d].astype(F32) for d in range(3)]

    def ahead_y(x):
        a = pltpu.roll(x, NZ, 1)
        return jnp.where(lane < NZ, a, pltpu.roll(a, last, 0))

    def behind_y(x):
        a = pltpu.roll(x, NZ, 1)
        return jnp.where(lane < NZ, pltpu.roll(a, 1, 0), a)

    flux = flux_of(opened[1], here, [ahead_y(x) for x in here], (line < last) | (lane < NZ))
    total = flux - behind_y(flux)
    flux = flux_of(
        opened[2], here, [pltpu.roll(x, LANES - 1, 1) for x in here], lane % NZ < NZ - 1
    )
    out_ref[...] = total + (flux - pltpu.roll(flux, 1, 1))

    @pl.when(has_up)
    def _():
        for c in to_up + [up_copy(g) for g in range(groups)]:
            c.wait_send()
        for at, dst in enumerate([zone_up] + [part(up, g) for g in range(groups)]):
            copy(dst, dst, base + at, me + 1).wait_recv()
        there = triple(up, zone_up)
        out_ref[...] += flux_of(open_ref[0].astype(F32), triple(fields_ref, zone_ref), there, True)

    @pl.when(has_down)
    def _():
        for c in to_down + [down_copy(g) for g in range(groups)]:
            c.wait_send()
        for at, dst in enumerate([zone_down, open_down] + [part(down, g) for g in range(groups)]):
            copy(dst, dst, at, me - 1).wait_recv()
        there = triple(down, zone_down)
        out_ref[...] -= flux_of(
            open_down[...].astype(F32), there, triple(fields_ref, zone_ref), True
        )


def mobility_of(s):
    return s * s / (s * s + 0.5 * (1.0 - s) * (1.0 - s))


def flux_of(opened, here, there, inside):
    p, m, k = here
    pn, mn, kn = there
    flux = opened * (2.0 * k * kn / (k + kn)) * 0.5 * (m + mn) * (p - pn)
    return jnp.where(inside, flux, 0.0)


def deliver_kernel(fields_ref, residual_ref, fields_out, residual_out, gone):
    stores = [
        pltpu.make_async_copy(src, dst, gone.at[k])
        for k, (src, dst) in enumerate([(fields_ref, fields_out), (residual_ref, residual_out)])
    ]
    for store in stores:
        store.start()
    for store in stores:
        store.wait()


def body(
    features,
    block_scale,
    spec_weight,
    bypass_weight,
    mlp_in,
    mlp_out,
    decode_weight,
    zone_ids,
    face_open,
    perm_table,
):
    width, rows, cells = features.shape
    n = lax.axis_size("gx")
    per = KYZ // n
    own = per * KX
    tall = cells // LANES
    zones = zone_ids.reshape(tall, LANES)
    opened = face_open.reshape(3, tall, LANES)
    flat = features.reshape(width, cells)
    table, turns, line = plane_table(), chunk_turns(), line_table(rows * n, per)
    hid = mlp_in.shape[0]
    shape = (n, per, 2 * width)
    block = pltpu.VMEM(shape, F32)
    sems = pltpu.SemaphoreType.DMA((n,))
    norm = 1.0 / (rows * n * NY * NZ)
    sources = (
        flat, block_scale.T, table, turns, *line, spec_weight,
        bypass_weight, mlp_in.T, mlp_out, decode_weight, zones, opened,
    )
    plane = pltpu.VMEM((tall, LANES), jnp.int32)
    near = pltpu.VMEM((2, tall, LANES), F32)
    groups = CHUNKS // GROUP
    links = pltpu.SemaphoreType.DMA((3 + 2 * groups,))
    fields, residual = pl.pallas_call(
        lambda *refs: mode_kernel(n, norm, *refs),
        out_shape=(
            pltpu.VMEM((2, tall, LANES), F32),
            pltpu.VMEM((tall, LANES), F32),
        ),
        in_specs=[pl.BlockSpec(memory_space=pltpu.HBM)] * (len(sources) + 1),
        out_specs=(VMEM, VMEM),
        scratch_shapes=[pltpu.VMEM(source.shape, source.dtype) for source in sources]
        + [
            pltpu.SMEM(perm_table.shape, F32),
            pltpu.VMEM((CHUNKS * width, CHUNK), BF16),
            pltpu.VMEM((CHUNKS // 2 * width, 2 * KYZ), BF16),
            pltpu.VMEM((2 * GROUP * width, CHUNK), BF16),
            pltpu.VMEM((2 * GROUP * hid, CHUNK), BF16),
            pltpu.VMEM((CHUNKS * width, CHUNK), F32),
            pltpu.VMEM((4 * GROUP, GROUP * hid), BF16),
            pltpu.VMEM((GROUP * hid, GROUP * width), BF16),
            pltpu.VMEM((GROUP * width, GROUP * width), BF16),
            near,
            near,
            plane,
            plane,
            plane,
            links,
            links,
            block,
            block,
            pltpu.VMEM((2 * width, own), F32),
            block,
            block,
            pltpu.SemaphoreType.DMA((len(sources) + groups,)),
            sems,
            sems,
            sems,
            sems,
        ],
        compiler_params=pltpu.CompilerParams(
            vmem_limit_bytes=60 << 20, collective_id=0, has_side_effects=True
        ),
        name="layer",
    )(*(pltpu.with_memory_space_constraint(x, pltpu.HBM) for x in (*sources, perm_table)))
    anywhere = pl.BlockSpec(memory_space=pl.ANY)
    fields, residual = pl.pallas_call(
        deliver_kernel,
        out_shape=(
            jax.ShapeDtypeStruct((2, tall, LANES), F32),
            jax.ShapeDtypeStruct((tall, LANES), F32),
        ),
        in_specs=[VMEM, VMEM],
        out_specs=(anywhere, anywhere),
        scratch_shapes=[pltpu.SemaphoreType.DMA((2,))],
        name="deliver",
    )(*(pltpu.with_memory_space_constraint(x, pltpu.VMEM) for x in (fields, residual)))
    return fields.reshape(2, rows, cells), residual.reshape(rows, cells)


def solution(mesh):
    in_specs = (
        P(None, ("groups", "gx"), None),
        P(None, ("groups", "gx")),
        P(None, None, None, "gx"),
        P(),
        P(),
        P(),
        P(),
        P(("groups", "gx"), None),
        P(None, ("groups", "gx"), None),
        P(),
    )
    out_specs = (P(None, ("groups", "gx"), None), P(("groups", "gx"), None))
    return jax.shard_map(body, mesh=mesh, in_specs=in_specs, out_specs=out_specs, check_vma=False)
```

```python
import math

import jax
import jax.numpy as jnp
import numpy as np
from jax import lax
from jax.experimental import pallas as pl
from jax.experimental.pallas import tpu as pltpu
from jax.sharding import PartitionSpec as P

NY = 512
NZ = 64
KX = 32
KY = 32
KZ = 8
ZONES = 8
YC = 16
LANES = 128
KYZ = KY * KZ
HALF = KYZ // 2
CHUNK = YC * NZ
CHUNKS = NY // YC
GROUP = 8
F32 = jnp.float32
BF16 = jnp.bfloat16
VMEM = pl.BlockSpec(memory_space=pltpu.VMEM)


def signed(count):
    steps = np.arange(count)
    return np.where(steps < count // 2, steps, steps - count)


def pair(table):
    high = table.astype(BF16)
    low = (table - high.astype(np.float64)).astype(BF16)
    return jnp.asarray(high), jnp.asarray(low)


def line_order(n):
    per, share = KYZ // n, KZ * n // KYZ
    parity, half, spot, i = np.indices((2, 2, n // 2, per // 2))
    device = (2 * (spot // share) + parity) * share + spot % share
    return (device * per + half * (per // 2) + i).reshape(-1)


def plane_table(order):
    ky, kz = signed(KY)[order // KZ][:, None], (order % KZ)[:, None]
    yy = np.repeat(np.arange(YC), NZ)[None]
    zz = np.tile(np.arange(NZ), YC)[None]
    angle = 2.0 * math.pi * ((ky * yy / NY + kz * zz / NZ) % 1.0)
    parts = [part[at : at + HALF] for at in (0, HALF) for part in (np.cos(angle), -np.sin(angle))]
    return jnp.asarray(np.concatenate(parts).astype(BF16))


def chunk_turns(order):
    ky = signed(KY)[order // KZ][None]
    angle = 2.0 * math.pi * ((ky * (YC * np.arange(CHUNKS))[:, None] / NY) % 1.0)
    return jnp.asarray(np.stack([np.cos(angle), np.sin(angle)]).astype(np.float32))


def line_table(total_x, lines):
    angle = 2.0 * math.pi * ((signed(KX)[None] * np.arange(total_x)[:, None] / total_x) % 1.0)
    same = np.eye(lines)
    parts = [
        np.einsum("xk,lm->xlmk", part, same).reshape(total_x * lines, lines * KX)
        for part in (np.cos(angle), np.sin(angle))
    ]
    return pair(np.concatenate(parts, axis=1))


def gelu_twice(x):
    x = x.astype(BF16)
    return x + x * jnp.tanh(x * (BF16(0.7978845608028654) + BF16(0.035677408136300125) * (x * x)))


def matmul(a, b, dims):
    return lax.dot_general(a, b, ((dims[:1], dims[1:]), ((), ())), preferred_element_type=F32)


def column(row):
    count = row.shape[1]
    shape = (count, count)
    same = lax.broadcasted_iota(jnp.int32, shape, 0) == lax.broadcasted_iota(jnp.int32, shape, 1)
    return jnp.sum(jnp.where(same, row, 0.0), axis=1, keepdims=True)


def scaled(cells, scale):
    return (cells.astype(F32) * scale).astype(BF16)


def split(x):
    high = x.astype(BF16)
    return high, (x - high.astype(F32)).astype(BF16)


def fine(a, table, dims):
    high, low = split(a)
    return (
        matmul(high, table[0], dims) + matmul(low, table[0], dims) + matmul(high, table[1], dims)
    )


def forward(f_ref, scale, table_ref, turn_ref, held, ready):
    width = f_ref.shape[0]
    real = [jnp.zeros((width, HALF), F32)] * 2
    imag = [jnp.zeros((width, HALF), F32)] * 2
    for first in range(0, CHUNKS, GROUP):
        ready(first // GROUP)
        for j in range(first, first + GROUP):
            held[j * width : (j + 1) * width, :] = scaled(
                f_ref[:, j * CHUNK : (j + 1) * CHUNK], scale
            )
        part = matmul(held[first * width : (first + GROUP) * width, :], table_ref[...], (1, 1))
        for j in range(first, first + GROUP):
            rows = part[(j - first) * width : (j - first + 1) * width]
            for h in range(2):
                at = h * HALF
                re, im = rows[:, 2 * at : 2 * at + HALF], rows[:, 2 * at + HALF : 2 * at + KYZ]
                c, s = (turn_ref[k, j : j + 1, at : at + HALF] for k in range(2))
                real[h] = real[h] + re * c + im * s
                imag[h] = imag[h] + im * c - re * s
    both = [jnp.concatenate([x, y], axis=0) for x, y in zip(real, imag)]
    quarter = HALF // 2
    tall = [jnp.concatenate([x[:, :quarter], x[:, quarter:]], axis=0) for x in both]
    return jnp.concatenate(tall, axis=1).T


def slot(device, n):
    share = KZ * n // KYZ
    ky = device // share
    return (ky % 2 * (KY // 2) + ky // 2) * share + device % share


def exchange(n, me, src, dst, place, spot, send_sem, recv_sem, meanwhile=None):
    def copy(d):
        peer = lax.rem(me + d, n)
        return pltpu.make_async_remote_copy(
            src_ref=src.at[place(peer)],
            dst_ref=dst.at[spot(me)],
            send_sem=send_sem.at[d],
            recv_sem=recv_sem.at[d],
            device_id={"gx": peer},
            device_id_type=pl.DeviceIdType.MESH,
        )

    def start(d, carry):
        copy(d).start()
        return carry

    def finish(d, carry):
        copy(d).wait()
        return carry

    lax.fori_loop(1, n, start, 0)
    dst[spot(me)] = src[place(me)]
    if meanwhile is not None:
        meanwhile()
    lax.fori_loop(1, n, finish, 0)


def one_hot(rows, cols, on_row, on_col):
    row = on_row(lax.broadcasted_iota(jnp.int32, (rows, cols), 0))
    col = on_col(lax.broadcasted_iota(jnp.int32, (rows, cols), 1))
    return jnp.where(row == col, 1.0, 0.0)


def block_diagonal(weight, rows, cols):
    tall = matmul(
        one_hot(GROUP * rows, rows, lambda r: r % rows, lambda c: c).astype(BF16), weight, (1, 0)
    ).astype(BF16)
    full = matmul(
        tall, one_hot(cols, GROUP * cols, lambda r: r, lambda c: c % cols).astype(BF16), (1, 0)
    )
    mask = one_hot(GROUP * rows, GROUP * cols, lambda r: r // rows, lambda c: c // cols)
    return (full * mask).astype(BF16)


def mode_kernel(
    n, norm, f_hbm, scale_hbm, table_hbm, turn_hbm, line_hbm, line_low_hbm, w_hbm,
    bypass_hbm, in_hbm, outw_hbm, dec_hbm, zone_hbm, open_hbm, perm_hbm, fields_ref, out_ref,
    f_ref, scale_ref, table_ref, turn_ref, line_ref, line_low, w_ref,
    bypass_ref, in_ref, outw_ref, dec_ref, zone_ref, open_ref, perm_ref,
    held, turned, lifted, hidden, skip, folded, wide_in, wide_by, up, down,
    perm_here, gate, perm_up, gate_down, cond, mob, send, recv,
    a_ref, lines, modes, back, landed, load_sem, send_a, recv_a, send_b, recv_b,
):
    me = lax.axis_index("gx")
    barrier = pltpu.get_barrier_semaphore()

    def greet(d, carry):
        pl.semaphore_signal(
            barrier, inc=1, device_id={"gx": lax.rem(me + d, n)},
            device_id_type=pl.DeviceIdType.MESH,
        )
        return carry

    lax.fori_loop(1, n, greet, 0)
    groups = CHUNKS // GROUP
    span = GROUP * CHUNK
    pieces = [
        (f_hbm.at[:, g * span : (g + 1) * span], f_ref.at[:, g * span : (g + 1) * span])
        for g in range(groups)
    ]
    wanted = [(table_hbm, table_ref), (scale_hbm, scale_ref), (turn_hbm, turn_ref)]
    wanted += pieces + [(line_hbm, line_ref), (line_low_hbm, line_low), (w_hbm, w_ref)]
    wanted += [(bypass_hbm, bypass_ref), (in_hbm, in_ref), (outw_hbm, outw_ref)]
    wanted += [(dec_hbm, dec_ref), (zone_hbm, zone_ref), (open_hbm, open_ref)]
    wanted += [(perm_hbm, perm_ref)]
    loads = [
        pltpu.make_async_copy(src, dst, load_sem.at[k]) for k, (src, dst) in enumerate(wanted)
    ]
    for load in loads:
        load.start()
    for load in loads[:3]:
        load.wait()
    scale = column(scale_ref[...])
    seen = forward(
        f_ref, scale, table_ref, turn_ref, held, lambda g: loads[3 + g].wait()
    )
    a_ref[...] = seen.reshape(a_ref.shape)
    pl.semaphore_wait(barrier, n - 1)

    def lookup(zones):
        total = jnp.zeros(zones.shape, F32)
        for zone in range(ZONES):
            total = jnp.where(zones == zone, perm_ref[zone], total)
        return total

    def weights():
        for load in loads[3 + groups :]:
            load.wait()
        perm_here[...] = lookup(zone_ref[...])
        gate[...] = open_ref[0].astype(F32) * perm_here[...]
        width, hid = in_ref.shape
        fold = jnp.dot(dec_ref[...], outw_ref[...], preferred_element_type=F32) * 0.5
        high = fold.astype(BF16).astype(F32)
        low = fold - high
        row = lax.broadcasted_iota(jnp.int32, (GROUP, hid), 0)
        for r in range(GROUP):
            rows = [
                jnp.where(row == r, part[k : k + 1, :], 0.0)
                for k in range(2)
                for part in (high, low)
            ]
            folded[:, r * hid : (r + 1) * hid] = jnp.concatenate(rows, axis=0).astype(BF16)
        wide_by[...] = block_diagonal(bypass_ref[...], width, width)
        wide_in[...] = block_diagonal(in_ref[...].T, hid, width) * BF16(0.5)
        tall_rows = GROUP * width

        def bypass(g, carry):
            rows = pl.ds(pl.multiple_of(g * tall_rows, tall_rows), tall_rows)
            skip[rows, :] = matmul(wide_by[...], held[rows, :], (1, 0))
            return carry

        lax.fori_loop(0, groups, bypass, 0)

    exchange(n, me, a_ref, lines, lambda d: slot(d, n), lambda d: d, send_a, recv_a, weights)
    has_up, has_down = me < n - 1, me > 0

    def copy(src, dst, at, peer):
        return pltpu.make_async_remote_copy(
            src_ref=src, dst_ref=dst, send_sem=send.at[at], recv_sem=recv.at[at],
            device_id={"gx": peer}, device_id_type=pl.DeviceIdType.MESH,
        )

    to_up = copy(gate, gate_down, 0, me + 1)
    to_down = copy(perm_here, perm_up, 1 + groups, me - 1)

    count, few, wide = lines.shape
    both = wide // 2
    width, own = both // 2, few * KX
    spread = fine(lines[...].reshape(count * few, wide), (line_ref[...], line_low[...]), (0, 0))
    for h in range(2):
        re, im = (spread[h * both + k * width : h * both + (k + 1) * width] for k in range(2))
        cols = slice(h * own, (h + 1) * own)
        modes[:width, cols] = re[:, :own] + im[:, own:]
        modes[width:, cols] = im[:, :own] - re[:, own:]

    def mix(i, carry):
        real, imag = carry
        re, im = modes[pl.ds(i, 1), :], modes[pl.ds(width + i, 1), :]
        wr, wi = w_ref[0, i].astype(F32), w_ref[1, i].astype(F32)
        return real + (re * wr - im * wi), imag + (re * wi + im * wr)

    zero = jnp.zeros((width, 2 * own), F32)
    real, imag = lax.fori_loop(0, width, mix, (zero, zero), unroll=4)
    line = me * 2 * few + lax.broadcasted_iota(jnp.int32, (1, 2 * own), 1) // KX
    weight = jnp.where(line % KZ == 0, norm, 2.0 * norm)
    real, imag = real * weight, imag * weight
    rows = []
    for h in range(2):
        re, im = (x[:, h * own : (h + 1) * own] for x in (real, imag))
        rows += [jnp.concatenate([re, -im], axis=1), jnp.concatenate([im, re], axis=1)]
    spun = jnp.concatenate(rows, axis=0)
    high, low = split(spun)
    turned_back = (
        matmul(line_ref[...], high, (1, 1))
        + matmul(line_ref[...], low, (1, 1))
        + matmul(line_low[...], high, (1, 1))
    )
    back[...] = turned_back.reshape(back.shape)
    tall = GROUP * CHUNK // LANES
    base = 1 + groups

    def part(ref, g):
        return ref.at[:, pl.ds(pl.multiple_of(g * tall, tall), tall)]

    def up_copy(g):
        return copy(part(fields_ref, g), part(down, g), 1 + g, me + 1)

    def down_copy(g):
        return copy(part(fields_ref, g), part(up, g), base + 1 + g, me - 1)

    shape = perm_here.shape
    last = shape[0] - 1
    lane = lax.broadcasted_iota(jnp.int32, shape, 1)
    line = lax.broadcasted_iota(jnp.int32, shape, 0)

    def ahead_y(x):
        a = pltpu.roll(x, NZ, 1)
        return jnp.where(lane < NZ, a, pltpu.roll(a, last, 0))

    def behind_y(x):
        a = pltpu.roll(x, NZ, 1)
        return jnp.where(lane < NZ, pltpu.roll(a, 1, 0), a)

    def ahead_z(x):
        return pltpu.roll(x, LANES - 1, 1)

    def conduct():
        @pl.when(has_up)
        def _():
            to_up.start()

        @pl.when(has_down)
        def _():
            to_down.start()

        k = perm_here[...]
        inside = (line < last) | (lane < NZ)
        cond[1] = jnp.where(inside, open_ref[1].astype(F32) * harmonic(k, ahead_y(k)), 0.0)
        cond[2] = jnp.where(
            lane % NZ < NZ - 1, open_ref[2].astype(F32) * harmonic(k, ahead_z(k)), 0.0
        )

    exchange(n, me, back, landed, lambda d: d, lambda d: slot(d, n), send_b, recv_b, conduct)
    across = landed[...].reshape(HALF, 4 * width).T
    quarter = HALF // 2
    re, im = (
        jnp.concatenate(
            [
                across[(2 * h + k) * width : (2 * h + k + 1) * width, p * quarter : (p + 1) * quarter]
                for p in range(2)
                for h in range(2)
            ],
            axis=1,
        )
        for k in range(2)
    )
    for j in range(CHUNKS // 2):
        c, s = turn_ref[0, j : j + 1, :], turn_ref[1, j : j + 1, :]
        spun_re, spun_im = (re * c - im * s).astype(BF16), (im * c + re * s).astype(BF16)
        for h in range(2):
            at = h * HALF
            rows = slice(j * width, (j + 1) * width)
            turned[rows, 2 * at : 2 * at + HALF] = spun_re[:, at : at + HALF]
            turned[rows, 2 * at + HALF : 2 * at + KYZ] = spun_im[:, at : at + HALF]
    tile = 2 * LANES
    hid = in_ref.shape[1]
    tall_rows, tall_hid, pairs = GROUP * width, GROUP * hid, groups // 2
    for g in range(pairs):
        low = slice(g * tall_rows, (g + 1) * tall_rows)
        high = slice((g + pairs) * tall_rows, (g + pairs + 1) * tall_rows)
        for at in range(0, CHUNK, tile):
            cols = slice(at, at + tile)
            even = matmul(turned[low, :KYZ], table_ref[:KYZ, cols], (1, 0))
            odd = matmul(turned[low, KYZ:], table_ref[KYZ:, cols], (1, 0))
            lifted[:tall_rows, cols] = gelu_twice(even + odd + skip[low, cols])
            lifted[tall_rows:, cols] = gelu_twice(even - odd + skip[high, cols])
        for k in range(2):
            at_g = g + k * pairs
            for at in range(0, CHUNK, tile):
                cols = slice(at, at + tile)
                hidden[k * tall_hid : (k + 1) * tall_hid, cols] = gelu_twice(
                    matmul(wide_in[...], lifted[k * tall_rows : (k + 1) * tall_rows, cols], (1, 0))
                )
            decoded = matmul(folded[...], hidden[k * tall_hid : (k + 1) * tall_hid, :], (1, 0))
            pressure = decoded[:GROUP] + decoded[GROUP : 2 * GROUP]
            saturation = jax.nn.sigmoid(decoded[2 * GROUP : 3 * GROUP] + decoded[3 * GROUP :])
            for r in range(CHUNK // LANES):
                where = pl.ds(at_g * tall + r, GROUP, stride=CHUNK // LANES)
                lanes = slice(r * LANES, (r + 1) * LANES)
                fields_ref[0, where, :] = pressure[:, lanes]
                fields_ref[1, where, :] = saturation[:, lanes]

            @pl.when(has_up)
            def _(at_g=at_g):
                up_copy(at_g).start()

            @pl.when(has_down)
            def _(at_g=at_g):
                down_copy(at_g).start()

    pressure, mobility = fields_ref[0], mobility_of(fields_ref[1])
    mob[...] = mobility
    flux = flux_of(cond[1], pressure, mobility, ahead_y(pressure), ahead_y(mobility))
    total = flux - behind_y(flux)
    flux = flux_of(cond[2], pressure, mobility, ahead_z(pressure), ahead_z(mobility))
    out_ref[...] = total + (flux - pltpu.roll(flux, 1, 1))
    @pl.when(has_up)
    def _():
        copy(perm_up, perm_up, base, me + 1).wait_recv()
        cond[0] = harmonic(gate[...], perm_up[...])

    @pl.when(has_down)
    def _():
        copy(gate_down, gate_down, 0, me - 1).wait_recv()
        cond[3] = harmonic(gate_down[...], perm_here[...])

    @pl.when(has_up)
    def _():
        for g in range(groups):
            copy(part(up, g), part(up, g), base + 1 + g, me + 1).wait_recv()
        out_ref[...] += flux_of(cond[0], fields_ref[0], mob[...], up[0], mobility_of(up[1]))

    @pl.when(has_down)
    def _():
        for g in range(groups):
            copy(part(down, g), part(down, g), 1 + g, me - 1).wait_recv()
        out_ref[...] -= flux_of(cond[3], down[0], mobility_of(down[1]), fields_ref[0], mob[...])

    @pl.when(has_up)
    def _():
        for c in [to_up] + [up_copy(g) for g in range(groups)]:
            c.wait_send()

    @pl.when(has_down)
    def _():
        for c in [to_down] + [down_copy(g) for g in range(groups)]:
            c.wait_send()


def mobility_of(s):
    return s * s / (s * s + 0.5 * (1.0 - s) * (1.0 - s))


def harmonic(a, b):
    return a * b / (a + b)


def flux_of(half, p, m, pn, mn):
    return half * (m + mn) * (p - pn)


def deliver_kernel(fields_ref, residual_ref, fields_out, residual_out, gone):
    stores = [
        pltpu.make_async_copy(src, dst, gone.at[k])
        for k, (src, dst) in enumerate([(fields_ref, fields_out), (residual_ref, residual_out)])
    ]
    for store in stores:
        store.start()
    for store in stores:
        store.wait()


def body(
    features,
    block_scale,
    spec_weight,
    bypass_weight,
    mlp_in,
    mlp_out,
    decode_weight,
    zone_ids,
    face_open,
    perm_table,
):
    width, rows, cells = features.shape
    n = lax.axis_size("gx")
    per = KYZ // n
    own = per * KX
    tall = cells // LANES
    zones = zone_ids.reshape(tall, LANES)
    opened = face_open.reshape(3, tall, LANES)
    flat = features.reshape(width, cells)
    order = line_order(n)
    table, turns, line = plane_table(order), chunk_turns(order), line_table(rows * n, per // 2)
    hid = mlp_in.shape[0]
    shape = (n, per // 2, 4 * width)
    block = pltpu.VMEM(shape, F32)
    sems = pltpu.SemaphoreType.DMA((n,))
    norm = 1.0 / (rows * n * NY * NZ)
    sources = (
        flat, block_scale.T, table, turns, *line, spec_weight,
        bypass_weight, mlp_in.T, mlp_out, decode_weight, zones, opened,
    )
    plane = pltpu.VMEM((tall, LANES), F32)
    near = pltpu.VMEM((2, tall, LANES), F32)
    groups = CHUNKS // GROUP
    links = pltpu.SemaphoreType.DMA((2 + 2 * groups,))
    fields, residual = pl.pallas_call(
        lambda *refs: mode_kernel(n, norm, *refs),
        out_shape=(
            pltpu.VMEM((2, tall, LANES), F32),
            pltpu.VMEM((tall, LANES), F32),
        ),
        in_specs=[pl.BlockSpec(memory_space=pltpu.HBM)] * (len(sources) + 1),
        out_specs=(VMEM, VMEM),
        scratch_shapes=[pltpu.VMEM(source.shape, source.dtype) for source in sources]
        + [
            pltpu.SMEM(perm_table.shape, F32),
            pltpu.VMEM((CHUNKS * width, CHUNK), BF16),
            pltpu.VMEM((CHUNKS // 2 * width, 2 * KYZ), BF16),
            pltpu.VMEM((2 * GROUP * width, CHUNK), BF16),
            pltpu.VMEM((2 * GROUP * hid, CHUNK), BF16),
            pltpu.VMEM((CHUNKS * width, CHUNK), F32),
            pltpu.VMEM((4 * GROUP, GROUP * hid), BF16),
            pltpu.VMEM((GROUP * hid, GROUP * width), BF16),
            pltpu.VMEM((GROUP * width, GROUP * width), BF16),
            near,
            near,
            plane,
            plane,
            plane,
            plane,
            pltpu.VMEM((4, tall, LANES), F32),
            plane,
            links,
            links,
            block,
            block,
            pltpu.VMEM((2 * width, own), F32),
            block,
            block,
            pltpu.SemaphoreType.DMA((len(sources) + groups,)),
            sems,
            sems,
            sems,
            sems,
        ],
        compiler_params=pltpu.CompilerParams(
            vmem_limit_bytes=60 << 20, collective_id=0, has_side_effects=True
        ),
        name="layer",
    )(*(pltpu.with_memory_space_constraint(x, pltpu.HBM) for x in (*sources, perm_table)))
    anywhere = pl.BlockSpec(memory_space=pl.ANY)
    fields, residual = pl.pallas_call(
        deliver_kernel,
        out_shape=(
            jax.ShapeDtypeStruct((2, tall, LANES), F32),
            jax.ShapeDtypeStruct((tall, LANES), F32),
        ),
        in_specs=[VMEM, VMEM],
        out_specs=(anywhere, anywhere),
        scratch_shapes=[pltpu.SemaphoreType.DMA((2,))],
        name="deliver",
    )(*(pltpu.with_memory_space_constraint(x, pltpu.VMEM) for x in (fields, residual)))
    return fields.reshape(2, rows, cells), residual.reshape(rows, cells)


def solution(mesh):
    in_specs = (
        P(None, ("groups", "gx"), None),
        P(None, ("groups", "gx")),
        P(None, None, None, "gx"),
        P(),
        P(),
        P(),
        P(),
        P(("groups", "gx"), None),
        P(None, ("groups", "gx"), None),
        P(),
    )
    out_specs = (P(None, ("groups", "gx"), None), P(("groups", "gx"), None))
    return jax.shard_map(body, mesh=mesh, in_specs=in_specs, out_specs=out_specs, check_vma=False)
```

```python
import math

import jax
import jax.numpy as jnp
import numpy as np
from jax import lax
from jax.experimental import pallas as pl
from jax.experimental.pallas import tpu as pltpu
from jax.sharding import PartitionSpec as P

NY = 512
NZ = 64
KX = 32
KY = 32
KZ = 8
ZONES = 8
YC = 16
LANES = 128
KYZ = KY * KZ
HALF = KYZ // 2
CHUNK = YC * NZ
CHUNKS = NY // YC
GROUP = 8
F32 = jnp.float32
BF16 = jnp.bfloat16
VMEM = pl.BlockSpec(memory_space=pltpu.VMEM)


def signed(count):
    steps = np.arange(count)
    return np.where(steps < count // 2, steps, steps - count)


def pair(table):
    high = table.astype(BF16)
    low = (table - high.astype(np.float64)).astype(BF16)
    return jnp.asarray(high), jnp.asarray(low)


def line_order(n):
    per, share = KYZ // n, KZ * n // KYZ
    parity, half, spot, i = np.indices((2, 2, n // 2, per // 2))
    device = (2 * (spot // share) + parity) * share + spot % share
    return (device * per + half * (per // 2) + i).reshape(-1)


def plane_table(order):
    ky, kz = signed(KY)[order // KZ][:, None], (order % KZ)[:, None]
    yy = np.repeat(np.arange(YC), NZ)[None]
    zz = np.tile(np.arange(NZ), YC)[None]
    angle = 2.0 * math.pi * ((ky * yy / NY + kz * zz / NZ) % 1.0)
    parts = [part[at : at + HALF] for at in (0, HALF) for part in (np.cos(angle), -np.sin(angle))]
    return pair(np.concatenate(parts))


def chunk_turns(order):
    ky = signed(KY)[order // KZ][None]
    angle = 2.0 * math.pi * ((ky * (YC * np.arange(CHUNKS))[:, None] / NY) % 1.0)
    return jnp.asarray(np.stack([np.cos(angle), np.sin(angle)]).astype(np.float32))


def line_table(total_x, lines):
    angle = 2.0 * math.pi * ((signed(KX)[None] * np.arange(total_x)[:, None] / total_x) % 1.0)
    same = np.eye(lines)
    parts = [
        np.einsum("xk,lm->xlmk", part, same).reshape(total_x * lines, lines * KX)
        for part in (np.cos(angle), np.sin(angle))
    ]
    return pair(np.concatenate(parts, axis=1))


def gelu_twice(x):
    x = x.astype(BF16)
    return x + x * jnp.tanh(x * (BF16(0.7978845608028654) + BF16(0.035677408136300125) * (x * x)))


def matmul(a, b, dims):
    return lax.dot_general(a, b, ((dims[:1], dims[1:]), ((), ())), preferred_element_type=F32)


def column(row):
    count = row.shape[1]
    shape = (count, count)
    same = lax.broadcasted_iota(jnp.int32, shape, 0) == lax.broadcasted_iota(jnp.int32, shape, 1)
    return jnp.sum(jnp.where(same, row, 0.0), axis=1, keepdims=True)


def scaled(cells, scale):
    return (cells.astype(F32) * scale).astype(BF16)


def split(x):
    high = x.astype(BF16)
    return high, (x - high.astype(F32)).astype(BF16)


def fine(a, table, dims):
    high, low = split(a)
    return (
        matmul(high, table[0], dims) + matmul(low, table[0], dims) + matmul(high, table[1], dims)
    )


def forward(f_ref, scale, table_ref, turn_ref, held, ready):
    width = f_ref.shape[0]
    real = [jnp.zeros((width, HALF), F32)] * 2
    imag = [jnp.zeros((width, HALF), F32)] * 2
    for first in range(0, CHUNKS, GROUP):
        ready(first // GROUP)
        for j in range(first, first + GROUP):
            held[j * width : (j + 1) * width, :] = scaled(
                f_ref[:, j * CHUNK : (j + 1) * CHUNK], scale
            )
        part = matmul(held[first * width : (first + GROUP) * width, :], table_ref[...], (1, 1))
        for j in range(first, first + GROUP):
            rows = part[(j - first) * width : (j - first + 1) * width]
            for h in range(2):
                at = h * HALF
                re, im = rows[:, 2 * at : 2 * at + HALF], rows[:, 2 * at + HALF : 2 * at + KYZ]
                c, s = (turn_ref[k, j : j + 1, at : at + HALF] for k in range(2))
                real[h] = real[h] + re * c + im * s
                imag[h] = imag[h] + im * c - re * s
    both = [jnp.concatenate([x, y], axis=0) for x, y in zip(real, imag)]
    quarter = HALF // 2
    tall = [jnp.concatenate([x[:, :quarter], x[:, quarter:]], axis=0) for x in both]
    return jnp.concatenate(tall, axis=1).T


def slot(device, n):
    share = KZ * n // KYZ
    ky = device // share
    return (ky % 2 * (KY // 2) + ky // 2) * share + device % share


def exchange(n, me, src, dst, place, spot, send_sem, recv_sem, meanwhile=None):
    def copy(d):
        peer = lax.rem(me + d, n)
        return pltpu.make_async_remote_copy(
            src_ref=src.at[place(peer)],
            dst_ref=dst.at[spot(me)],
            send_sem=send_sem.at[d],
            recv_sem=recv_sem.at[d],
            device_id={"gx": peer},
            device_id_type=pl.DeviceIdType.MESH,
        )

    def start(d, carry):
        copy(d).start()
        return carry

    def finish(d, carry):
        copy(d).wait()
        return carry

    lax.fori_loop(1, n, start, 0)
    dst[spot(me)] = src[place(me)]
    if meanwhile is not None:
        meanwhile()
    lax.fori_loop(1, n, finish, 0)


def one_hot(rows, cols, on_row, on_col):
    row = on_row(lax.broadcasted_iota(jnp.int32, (rows, cols), 0))
    col = on_col(lax.broadcasted_iota(jnp.int32, (rows, cols), 1))
    return jnp.where(row == col, 1.0, 0.0)


def block_diagonal(weight, rows, cols):
    tall = matmul(
        one_hot(GROUP * rows, rows, lambda r: r % rows, lambda c: c).astype(BF16), weight, (1, 0)
    ).astype(BF16)
    full = matmul(
        tall, one_hot(cols, GROUP * cols, lambda r: r, lambda c: c % cols).astype(BF16), (1, 0)
    )
    mask = one_hot(GROUP * rows, GROUP * cols, lambda r: r // rows, lambda c: c // cols)
    return (full * mask).astype(BF16)


def mode_kernel(
    n, norm, f_hbm, scale_hbm, table_hbm, turn_hbm, line_hbm, line_low_hbm, w_hbm,
    bypass_hbm, in_hbm, outw_hbm, dec_hbm, zone_hbm, open_hbm, perm_hbm, fine_hbm, fields_ref, out_ref,
    f_ref, scale_ref, table_ref, turn_ref, line_ref, line_low, w_ref,
    bypass_ref, in_ref, outw_ref, dec_ref, zone_ref, open_ref, perm_ref, fine_ref,
    held, turned, lifted, hidden, skip, folded, wide_in, wide_by, up, down,
    perm_here, gate, perm_up, gate_down, cond, mob, send, recv,
    a_ref, lines, modes, back, landed, load_sem, send_a, recv_a, send_b, recv_b,
):
    me = lax.axis_index("gx")
    barrier = pltpu.get_barrier_semaphore()

    def greet(d, carry):
        pl.semaphore_signal(
            barrier, inc=1, device_id={"gx": lax.rem(me + d, n)},
            device_id_type=pl.DeviceIdType.MESH,
        )
        return carry

    lax.fori_loop(1, n, greet, 0)
    groups = CHUNKS // GROUP
    span = GROUP * CHUNK
    pieces = [
        (f_hbm.at[:, g * span : (g + 1) * span], f_ref.at[:, g * span : (g + 1) * span])
        for g in range(groups)
    ]
    wanted = [(table_hbm, table_ref), (scale_hbm, scale_ref), (turn_hbm, turn_ref)]
    wanted += pieces + [(line_hbm, line_ref), (line_low_hbm, line_low), (w_hbm, w_ref)]
    wanted += [(bypass_hbm, bypass_ref), (in_hbm, in_ref), (outw_hbm, outw_ref)]
    wanted += [(dec_hbm, dec_ref), (zone_hbm, zone_ref), (open_hbm, open_ref)]
    wanted += [(perm_hbm, perm_ref), (fine_hbm, fine_ref)]
    loads = [
        pltpu.make_async_copy(src, dst, load_sem.at[k]) for k, (src, dst) in enumerate(wanted)
    ]
    for load in loads:
        load.start()
    for load in loads[:3]:
        load.wait()
    scale = column(scale_ref[...])
    seen = forward(
        f_ref, scale, table_ref, turn_ref, held, lambda g: loads[3 + g].wait()
    )
    a_ref[...] = seen.reshape(a_ref.shape)
    pl.semaphore_wait(barrier, n - 1)

    def lookup(zones):
        total = jnp.zeros(zones.shape, F32)
        for zone in range(ZONES):
            total = jnp.where(zones == zone, perm_ref[zone], total)
        return total

    def weights():
        for load in loads[3 + groups :]:
            load.wait()
        perm_here[...] = lookup(zone_ref[...])
        gate[...] = open_ref[0].astype(F32) * perm_here[...]
        width, hid = in_ref.shape
        fold = jnp.dot(dec_ref[...], outw_ref[...], preferred_element_type=F32) * 0.5
        high = fold.astype(BF16).astype(F32)
        low = fold - high
        row = lax.broadcasted_iota(jnp.int32, (GROUP, hid), 0)
        for r in range(GROUP):
            rows = [
                jnp.where(row == r, part[k : k + 1, :], 0.0)
                for k in range(2)
                for part in (high, low)
            ]
            folded[:, r * hid : (r + 1) * hid] = jnp.concatenate(rows, axis=0).astype(BF16)
        wide_by[...] = block_diagonal(bypass_ref[...], width, width)
        wide_in[...] = block_diagonal(in_ref[...].T, hid, width) * BF16(0.5)
        tall_rows = GROUP * width

        def bypass(g, carry):
            rows = pl.ds(pl.multiple_of(g * tall_rows, tall_rows), tall_rows)
            skip[rows, :] = matmul(wide_by[...], held[rows, :], (1, 0))
            return carry

        lax.fori_loop(0, groups, bypass, 0)

    exchange(n, me, a_ref, lines, lambda d: slot(d, n), lambda d: d, send_a, recv_a, weights)
    has_up, has_down = me < n - 1, me > 0

    def copy(src, dst, at, peer):
        return pltpu.make_async_remote_copy(
            src_ref=src, dst_ref=dst, send_sem=send.at[at], recv_sem=recv.at[at],
            device_id={"gx": peer}, device_id_type=pl.DeviceIdType.MESH,
        )

    to_up = copy(gate, gate_down, 0, me + 1)
    to_down = copy(perm_here, perm_up, 1 + groups, me - 1)

    count, few, wide = lines.shape
    both = wide // 2
    width, own = both // 2, few * KX
    spread = fine(lines[...].reshape(count * few, wide), (line_ref[...], line_low[...]), (0, 0))
    for h in range(2):
        re, im = (spread[h * both + k * width : h * both + (k + 1) * width] for k in range(2))
        cols = slice(h * own, (h + 1) * own)
        modes[:width, cols] = re[:, :own] + im[:, own:]
        modes[width:, cols] = im[:, :own] - re[:, own:]

    def mix(i, carry):
        real, imag = carry
        re, im = modes[pl.ds(i, 1), :], modes[pl.ds(width + i, 1), :]
        wr, wi = w_ref[0, i].astype(F32), w_ref[1, i].astype(F32)
        return real + (re * wr - im * wi), imag + (re * wi + im * wr)

    zero = jnp.zeros((width, 2 * own), F32)
    real, imag = lax.fori_loop(0, width, mix, (zero, zero), unroll=4)
    line = me * 2 * few + lax.broadcasted_iota(jnp.int32, (1, 2 * own), 1) // KX
    weight = jnp.where(line % KZ == 0, norm, 2.0 * norm)
    real, imag = real * weight, imag * weight
    rows = []
    for h in range(2):
        re, im = (x[:, h * own : (h + 1) * own] for x in (real, imag))
        rows += [jnp.concatenate([re, -im], axis=1), jnp.concatenate([im, re], axis=1)]
    spun = jnp.concatenate(rows, axis=0)
    high, low = split(spun)
    turned_back = (
        matmul(line_ref[...], high, (1, 1))
        + matmul(line_ref[...], low, (1, 1))
        + matmul(line_low[...], high, (1, 1))
    )
    back[...] = turned_back.reshape(back.shape)
    tall = GROUP * CHUNK // LANES
    base = 1 + groups

    def part(ref, g):
        return ref.at[:, pl.ds(pl.multiple_of(g * tall, tall), tall)]

    def up_copy(g):
        return copy(part(fields_ref, g), part(down, g), 1 + g, me + 1)

    def down_copy(g):
        return copy(part(fields_ref, g), part(up, g), base + 1 + g, me - 1)

    shape = perm_here.shape
    last = shape[0] - 1
    lane = lax.broadcasted_iota(jnp.int32, shape, 1)
    line = lax.broadcasted_iota(jnp.int32, shape, 0)

    def ahead_y(x):
        a = pltpu.roll(x, NZ, 1)
        return jnp.where(lane < NZ, a, pltpu.roll(a, last, 0))

    def behind_y(x):
        a = pltpu.roll(x, NZ, 1)
        return jnp.where(lane < NZ, pltpu.roll(a, 1, 0), a)

    def ahead_z(x):
        return pltpu.roll(x, LANES - 1, 1)

    def conduct():
        @pl.when(has_up)
        def _():
            to_up.start()

        @pl.when(has_down)
        def _():
            to_down.start()

        k = perm_here[...]
        inside = (line < last) | (lane < NZ)
        cond[1] = jnp.where(inside, open_ref[1].astype(F32) * harmonic(k, ahead_y(k)), 0.0)
        cond[2] = jnp.where(
            lane % NZ < NZ - 1, open_ref[2].astype(F32) * harmonic(k, ahead_z(k)), 0.0
        )

    exchange(n, me, back, landed, lambda d: d, lambda d: slot(d, n), send_b, recv_b, conduct)
    across = landed[...].reshape(HALF, 4 * width).T
    quarter = HALF // 2
    re, im = (
        jnp.concatenate(
            [
                across[(2 * h + k) * width : (2 * h + k + 1) * width, p * quarter : (p + 1) * quarter]
                for p in range(2)
                for h in range(2)
            ],
            axis=1,
        )
        for k in range(2)
    )
    for j in range(CHUNKS // 2):
        c, s = turn_ref[0, j : j + 1, :], turn_ref[1, j : j + 1, :]
        spun_re, spun_im = split(re * c - im * s), split(im * c + re * s)
        for h in range(2):
            at = h * HALF
            rows = slice(j * width, (j + 1) * width)
            for k in range(2):
                turned[k, rows, 2 * at : 2 * at + HALF] = spun_re[k][:, at : at + HALF]
                turned[k, rows, 2 * at + HALF : 2 * at + KYZ] = spun_im[k][:, at : at + HALF]
    tile = 2 * LANES
    hid = in_ref.shape[1]
    tall_rows, tall_hid, pairs = GROUP * width, GROUP * hid, groups // 2
    for g in range(pairs):
        low = slice(g * tall_rows, (g + 1) * tall_rows)
        high = slice((g + pairs) * tall_rows, (g + pairs + 1) * tall_rows)
        for at in range(0, CHUNK, tile):
            cols = slice(at, at + tile)
            even, odd = (
                matmul(turned[0, low, side], table_ref[side, cols], (1, 0))
                + matmul(turned[1, low, side], table_ref[side, cols], (1, 0))
                + matmul(turned[0, low, side], fine_ref[side, cols], (1, 0))
                for side in (slice(0, KYZ), slice(KYZ, 2 * KYZ))
            )
            lifted[:tall_rows, cols] = gelu_twice(even + odd + skip[low, cols])
            lifted[tall_rows:, cols] = gelu_twice(even - odd + skip[high, cols])
        for k in range(2):
            at_g = g + k * pairs
            for at in range(0, CHUNK, tile):
                cols = slice(at, at + tile)
                hidden[k * tall_hid : (k + 1) * tall_hid, cols] = gelu_twice(
                    matmul(wide_in[...], lifted[k * tall_rows : (k + 1) * tall_rows, cols], (1, 0))
                )
            decoded = matmul(folded[...], hidden[k * tall_hid : (k + 1) * tall_hid, :], (1, 0))
            pressure = decoded[:GROUP] + decoded[GROUP : 2 * GROUP]
            saturation = jax.nn.sigmoid(decoded[2 * GROUP : 3 * GROUP] + decoded[3 * GROUP :])
            for r in range(CHUNK // LANES):
                where = pl.ds(at_g * tall + r, GROUP, stride=CHUNK // LANES)
                lanes = slice(r * LANES, (r + 1) * LANES)
                fields_ref[0, where, :] = pressure[:, lanes]
                fields_ref[1, where, :] = saturation[:, lanes]

            @pl.when(has_up)
            def _(at_g=at_g):
                up_copy(at_g).start()

            @pl.when(has_down)
            def _(at_g=at_g):
                down_copy(at_g).start()

    pressure, mobility = fields_ref[0], mobility_of(fields_ref[1])
    mob[...] = mobility
    flux = flux_of(cond[1], pressure, mobility, ahead_y(pressure), ahead_y(mobility))
    total = flux - behind_y(flux)
    flux = flux_of(cond[2], pressure, mobility, ahead_z(pressure), ahead_z(mobility))
    out_ref[...] = total + (flux - pltpu.roll(flux, 1, 1))
    @pl.when(has_up)
    def _():
        copy(perm_up, perm_up, base, me + 1).wait_recv()
        cond[0] = harmonic(gate[...], perm_up[...])

    @pl.when(has_down)
    def _():
        copy(gate_down, gate_down, 0, me - 1).wait_recv()
        cond[3] = harmonic(gate_down[...], perm_here[...])

    @pl.when(has_up)
    def _():
        for g in range(groups):
            copy(part(up, g), part(up, g), base + 1 + g, me + 1).wait_recv()
        out_ref[...] += flux_of(cond[0], fields_ref[0], mob[...], up[0], mobility_of(up[1]))

    @pl.when(has_down)
    def _():
        for g in range(groups):
            copy(part(down, g), part(down, g), 1 + g, me - 1).wait_recv()
        out_ref[...] -= flux_of(cond[3], down[0], mobility_of(down[1]), fields_ref[0], mob[...])

    @pl.when(has_up)
    def _():
        for c in [to_up] + [up_copy(g) for g in range(groups)]:
            c.wait_send()

    @pl.when(has_down)
    def _():
        for c in [to_down] + [down_copy(g) for g in range(groups)]:
            c.wait_send()


def mobility_of(s):
    return s * s / (s * s + 0.5 * (1.0 - s) * (1.0 - s))


def harmonic(a, b):
    return a * b / (a + b)


def flux_of(half, p, m, pn, mn):
    return half * (m + mn) * (p - pn)


def deliver_kernel(fields_ref, residual_ref, fields_out, residual_out, gone):
    stores = [
        pltpu.make_async_copy(src, dst, gone.at[k])
        for k, (src, dst) in enumerate([(fields_ref, fields_out), (residual_ref, residual_out)])
    ]
    for store in stores:
        store.start()
    for store in stores:
        store.wait()


def body(
    features,
    block_scale,
    spec_weight,
    bypass_weight,
    mlp_in,
    mlp_out,
    decode_weight,
    zone_ids,
    face_open,
    perm_table,
):
    width, rows, cells = features.shape
    n = lax.axis_size("gx")
    per = KYZ // n
    own = per * KX
    tall = cells // LANES
    zones = zone_ids.reshape(tall, LANES)
    opened = face_open.reshape(3, tall, LANES)
    flat = features.reshape(width, cells)
    order = line_order(n)
    table, turns, line = plane_table(order), chunk_turns(order), line_table(rows * n, per // 2)
    hid = mlp_in.shape[0]
    shape = (n, per // 2, 4 * width)
    block = pltpu.VMEM(shape, F32)
    sems = pltpu.SemaphoreType.DMA((n,))
    norm = 1.0 / (rows * n * NY * NZ)
    sources = (
        flat, block_scale.T, table[0], turns, *line, spec_weight,
        bypass_weight, mlp_in.T, mlp_out, decode_weight, zones, opened, perm_table, table[1],
    )
    plane = pltpu.VMEM((tall, LANES), F32)
    near = pltpu.VMEM((2, tall, LANES), F32)
    groups = CHUNKS // GROUP
    links = pltpu.SemaphoreType.DMA((2 + 2 * groups,))
    fields, residual = pl.pallas_call(
        lambda *refs: mode_kernel(n, norm, *refs),
        out_shape=(
            pltpu.VMEM((2, tall, LANES), F32),
            pltpu.VMEM((tall, LANES), F32),
        ),
        in_specs=[pl.BlockSpec(memory_space=pltpu.HBM)] * len(sources),
        out_specs=(VMEM, VMEM),
        scratch_shapes=[
            (pltpu.SMEM if source is perm_table else pltpu.VMEM)(source.shape, source.dtype)
            for source in sources
        ]
        + [
            pltpu.VMEM((CHUNKS * width, CHUNK), BF16),
            pltpu.VMEM((2, CHUNKS // 2 * width, 2 * KYZ), BF16),
            pltpu.VMEM((2 * GROUP * width, CHUNK), BF16),
            pltpu.VMEM((2 * GROUP * hid, CHUNK), BF16),
            pltpu.VMEM((CHUNKS * width, CHUNK), F32),
            pltpu.VMEM((4 * GROUP, GROUP * hid), BF16),
            pltpu.VMEM((GROUP * hid, GROUP * width), BF16),
            pltpu.VMEM((GROUP * width, GROUP * width), BF16),
            near,
            near,
            plane,
            plane,
            plane,
            plane,
            pltpu.VMEM((4, tall, LANES), F32),
            plane,
            links,
            links,
            block,
            block,
            pltpu.VMEM((2 * width, own), F32),
            block,
            block,
            pltpu.SemaphoreType.DMA((len(sources) + groups,)),
            sems,
            sems,
            sems,
            sems,
        ],
        compiler_params=pltpu.CompilerParams(
            vmem_limit_bytes=60 << 20, collective_id=0, has_side_effects=True
        ),
        name="layer",
    )(*(pltpu.with_memory_space_constraint(x, pltpu.HBM) for x in sources))
    anywhere = pl.BlockSpec(memory_space=pl.ANY)
    fields, residual = pl.pallas_call(
        deliver_kernel,
        out_shape=(
            jax.ShapeDtypeStruct((2, tall, LANES), F32),
            jax.ShapeDtypeStruct((tall, LANES), F32),
        ),
        in_specs=[VMEM, VMEM],
        out_specs=(anywhere, anywhere),
        scratch_shapes=[pltpu.SemaphoreType.DMA((2,))],
        name="deliver",
    )(*(pltpu.with_memory_space_constraint(x, pltpu.VMEM) for x in (fields, residual)))
    return fields.reshape(2, rows, cells), residual.reshape(rows, cells)


def solution(mesh):
    in_specs = (
        P(None, ("groups", "gx"), None),
        P(None, ("groups", "gx")),
        P(None, None, None, "gx"),
        P(),
        P(),
        P(),
        P(),
        P(("groups", "gx"), None),
        P(None, ("groups", "gx"), None),
        P(),
    )
    out_specs = (P(None, ("groups", "gx"), None), P(("groups", "gx"), None))
    return jax.shard_map(body, mesh=mesh, in_specs=in_specs, out_specs=out_specs, check_vma=False)
```

```python
import math

import jax
import jax.numpy as jnp
import numpy as np
from jax import lax
from jax.experimental import pallas as pl
from jax.experimental.pallas import tpu as pltpu
from jax.sharding import PartitionSpec as P

NY = 512
NZ = 64
KX = 32
KY = 32
KZ = 8
ZONES = 8
YC = 16
LANES = 128
KYZ = KY * KZ
HALF = KYZ // 2
CHUNK = YC * NZ
CHUNKS = NY // YC
GROUP = 8
F32 = jnp.float32
BF16 = jnp.bfloat16
VMEM = pl.BlockSpec(memory_space=pltpu.VMEM)


def signed(count):
    steps = np.arange(count)
    return np.where(steps < count // 2, steps, steps - count)


def pair(table):
    high = table.astype(BF16)
    low = (table - high.astype(np.float64)).astype(BF16)
    return jnp.asarray(high), jnp.asarray(low)


def line_order(n):
    per, share = KYZ // n, KZ * n // KYZ
    parity, half, spot, i = np.indices((2, 2, n // 2, per // 2))
    device = (2 * (spot // share) + parity) * share + spot % share
    return (device * per + half * (per // 2) + i).reshape(-1)


def plane_table(order):
    ky, kz = signed(KY)[order // KZ][:, None], (order % KZ)[:, None]
    yy = np.repeat(np.arange(YC), NZ)[None]
    zz = np.tile(np.arange(NZ), YC)[None]
    angle = 2.0 * math.pi * ((ky * yy / NY + kz * zz / NZ) % 1.0)
    parts = [part[at : at + HALF] for at in (0, HALF) for part in (np.cos(angle), -np.sin(angle))]
    return pair(np.concatenate(parts))


def chunk_turns(order):
    ky = signed(KY)[order // KZ][None]
    angle = 2.0 * math.pi * ((ky * (YC * np.arange(CHUNKS))[:, None] / NY) % 1.0)
    return jnp.asarray(np.stack([np.cos(angle), np.sin(angle)]).astype(np.float32))


def line_table(total_x, lines):
    angle = 2.0 * math.pi * ((signed(KX)[None] * np.arange(total_x)[:, None] / total_x) % 1.0)
    same = np.eye(lines)
    parts = [
        np.einsum("xk,lm->xlmk", part, same).reshape(total_x * lines, lines * KX)
        for part in (np.cos(angle), np.sin(angle))
    ]
    return pair(np.concatenate(parts, axis=1))


def gelu_twice(x):
    x = x.astype(BF16)
    return x + x * jnp.tanh(x * (BF16(0.7978845608028654) + BF16(0.035677408136300125) * (x * x)))


def matmul(a, b, dims):
    return lax.dot_general(a, b, ((dims[:1], dims[1:]), ((), ())), preferred_element_type=F32)


def column(row):
    count = row.shape[1]
    shape = (count, count)
    same = lax.broadcasted_iota(jnp.int32, shape, 0) == lax.broadcasted_iota(jnp.int32, shape, 1)
    return jnp.sum(jnp.where(same, row, 0.0), axis=1, keepdims=True)


def scaled(cells, scale):
    return (cells.astype(F32) * scale).astype(BF16)


def split(x):
    high = x.astype(BF16)
    return high, (x - high.astype(F32)).astype(BF16)


def fine(a, table, dims):
    high, low = split(a)
    return (
        matmul(high, table[0], dims) + matmul(low, table[0], dims) + matmul(high, table[1], dims)
    )


def forward(f_ref, scale, table_ref, turn_ref, held, ready):
    width = f_ref.shape[0]
    real = [jnp.zeros((width, HALF), F32)] * 2
    imag = [jnp.zeros((width, HALF), F32)] * 2
    for first in range(0, CHUNKS, GROUP):
        ready(first // GROUP)
        for j in range(first, first + GROUP):
            held[j * width : (j + 1) * width, :] = scaled(
                f_ref[:, j * CHUNK : (j + 1) * CHUNK], scale
            )
        part = matmul(held[first * width : (first + GROUP) * width, :], table_ref[...], (1, 1))
        for j in range(first, first + GROUP):
            rows = part[(j - first) * width : (j - first + 1) * width]
            for h in range(2):
                at = h * HALF
                re, im = rows[:, 2 * at : 2 * at + HALF], rows[:, 2 * at + HALF : 2 * at + KYZ]
                c, s = (turn_ref[k, j : j + 1, at : at + HALF] for k in range(2))
                real[h] = real[h] + re * c + im * s
                imag[h] = imag[h] + im * c - re * s
    both = [jnp.concatenate([x, y], axis=0) for x, y in zip(real, imag)]
    quarter = HALF // 2
    tall = [jnp.concatenate([x[:, :quarter], x[:, quarter:]], axis=0) for x in both]
    return jnp.concatenate(tall, axis=1).T


def slot(device, n):
    share = KZ * n // KYZ
    ky = device // share
    return (ky % 2 * (KY // 2) + ky // 2) * share + device % share


def exchange(n, me, src, dst, place, spot, send_sem, recv_sem, meanwhile=None):
    def copy(d):
        peer = lax.rem(me + d, n)
        return pltpu.make_async_remote_copy(
            src_ref=src.at[place(peer)],
            dst_ref=dst.at[spot(me)],
            send_sem=send_sem,
            recv_sem=recv_sem,
            device_id={"gx": peer},
            device_id_type=pl.DeviceIdType.MESH,
        )

    def start(d, carry):
        copy(d).start()
        return carry

    lax.fori_loop(1, n, start, 0)
    dst[spot(me)] = src[place(me)]
    if meanwhile is not None:
        meanwhile()
    landing = dst.at[pl.ds(0, n - 1)]
    pltpu.make_async_copy(landing, landing, recv_sem).wait()
    return pltpu.make_async_copy(landing, landing, send_sem)


def one_hot(rows, cols, on_row, on_col):
    row = on_row(lax.broadcasted_iota(jnp.int32, (rows, cols), 0))
    col = on_col(lax.broadcasted_iota(jnp.int32, (rows, cols), 1))
    return jnp.where(row == col, 1.0, 0.0)


def block_diagonal(weight, rows, cols):
    tall = matmul(
        one_hot(GROUP * rows, rows, lambda r: r % rows, lambda c: c).astype(BF16), weight, (1, 0)
    ).astype(BF16)
    full = matmul(
        tall, one_hot(cols, GROUP * cols, lambda r: r, lambda c: c % cols).astype(BF16), (1, 0)
    )
    mask = one_hot(GROUP * rows, GROUP * cols, lambda r: r // rows, lambda c: c // cols)
    return (full * mask).astype(BF16)


def mode_kernel(
    n, norm, f_hbm, scale_hbm, table_hbm, turn_hbm, line_hbm, line_low_hbm, w_hbm,
    bypass_hbm, in_hbm, outw_hbm, dec_hbm, zone_hbm, open_hbm, perm_hbm, fine_hbm, fields_ref, out_ref,
    f_ref, scale_ref, table_ref, turn_ref, line_ref, line_low, w_ref,
    bypass_ref, in_ref, outw_ref, dec_ref, zone_ref, open_ref, perm_ref, fine_ref,
    held, turned, lifted, hidden, skip, folded, wide_in, wide_by, up, down,
    perm_here, gate, perm_up, gate_down, cond, mob, send, recv,
    a_ref, lines, modes, back, landed, load_sem, send_a, recv_a, send_b, recv_b,
):
    me = lax.axis_index("gx")
    barrier = pltpu.get_barrier_semaphore()

    def greet(d, carry):
        pl.semaphore_signal(
            barrier, inc=1, device_id={"gx": lax.rem(me + d, n)},
            device_id_type=pl.DeviceIdType.MESH,
        )
        return carry

    lax.fori_loop(1, n, greet, 0)
    groups = CHUNKS // GROUP
    span = GROUP * CHUNK
    pieces = [
        (f_hbm.at[:, g * span : (g + 1) * span], f_ref.at[:, g * span : (g + 1) * span])
        for g in range(groups)
    ]
    wanted = [(table_hbm, table_ref), (scale_hbm, scale_ref), (turn_hbm, turn_ref)]
    wanted += pieces + [(line_hbm, line_ref), (line_low_hbm, line_low), (w_hbm, w_ref)]
    wanted += [(bypass_hbm, bypass_ref), (in_hbm, in_ref), (outw_hbm, outw_ref)]
    wanted += [(dec_hbm, dec_ref), (zone_hbm, zone_ref), (open_hbm, open_ref)]
    wanted += [(perm_hbm, perm_ref), (fine_hbm, fine_ref)]
    loads = [
        pltpu.make_async_copy(src, dst, load_sem.at[k]) for k, (src, dst) in enumerate(wanted)
    ]
    for load in loads:
        load.start()
    for load in loads[:3]:
        load.wait()
    scale = column(scale_ref[...])
    seen = forward(
        f_ref, scale, table_ref, turn_ref, held, lambda g: loads[3 + g].wait()
    )
    a_ref[...] = seen.reshape(a_ref.shape)
    pl.semaphore_wait(barrier, n - 1)

    def lookup(zones):
        total = jnp.zeros(zones.shape, F32)
        for zone in range(ZONES):
            total = jnp.where(zones == zone, perm_ref[zone], total)
        return total

    def weights():
        for load in loads[3 + groups :]:
            load.wait()
        perm_here[...] = lookup(zone_ref[...])
        gate[...] = open_ref[0].astype(F32) * perm_here[...]
        width, hid = in_ref.shape
        fold = jnp.dot(dec_ref[...], outw_ref[...], preferred_element_type=F32) * 0.5
        high = fold.astype(BF16).astype(F32)
        low = fold - high
        row = lax.broadcasted_iota(jnp.int32, (GROUP, hid), 0)
        for r in range(GROUP):
            rows = [
                jnp.where(row == r, part[k : k + 1, :], 0.0)
                for k in range(2)
                for part in (high, low)
            ]
            folded[:, r * hid : (r + 1) * hid] = jnp.concatenate(rows, axis=0).astype(BF16)
        wide_by[...] = block_diagonal(bypass_ref[...], width, width)
        wide_in[...] = block_diagonal(in_ref[...].T, hid, width) * BF16(0.5)
        tall_rows = GROUP * width

        def bypass(g, carry):
            rows = pl.ds(pl.multiple_of(g * tall_rows, tall_rows), tall_rows)
            skip[rows, :] = matmul(wide_by[...], held[rows, :], (1, 0))
            return carry

        lax.fori_loop(0, groups, bypass, 0)

    sent = exchange(n, me, a_ref, lines, lambda d: slot(d, n), lambda d: d, send_a, recv_a, weights)
    has_up, has_down = me < n - 1, me > 0

    def copy(src, dst, at, peer):
        return pltpu.make_async_remote_copy(
            src_ref=src, dst_ref=dst, send_sem=send.at[at], recv_sem=recv.at[at],
            device_id={"gx": peer}, device_id_type=pl.DeviceIdType.MESH,
        )

    to_up = copy(gate, gate_down, 0, me + 1)
    to_down = copy(perm_here, perm_up, 1 + groups, me - 1)

    count, few, wide = lines.shape
    both = wide // 2
    width, own = both // 2, few * KX
    spread = fine(lines[...].reshape(count * few, wide), (line_ref[...], line_low[...]), (0, 0))
    for h in range(2):
        re, im = (spread[h * both + k * width : h * both + (k + 1) * width] for k in range(2))
        cols = slice(h * own, (h + 1) * own)
        modes[:width, cols] = re[:, :own] + im[:, own:]
        modes[width:, cols] = im[:, :own] - re[:, own:]

    def mix(i, carry):
        real, imag = carry
        re, im = modes[pl.ds(i, 1), :], modes[pl.ds(width + i, 1), :]
        wr, wi = w_ref[0, i].astype(F32), w_ref[1, i].astype(F32)
        return real + (re * wr - im * wi), imag + (re * wi + im * wr)

    zero = jnp.zeros((width, 2 * own), F32)
    real, imag = lax.fori_loop(0, width, mix, (zero, zero), unroll=4)
    line = me * 2 * few + lax.broadcasted_iota(jnp.int32, (1, 2 * own), 1) // KX
    weight = jnp.where(line % KZ == 0, norm, 2.0 * norm)
    real, imag = real * weight, imag * weight
    rows = []
    for h in range(2):
        re, im = (x[:, h * own : (h + 1) * own] for x in (real, imag))
        rows += [jnp.concatenate([re, -im], axis=1), jnp.concatenate([im, re], axis=1)]
    spun = jnp.concatenate(rows, axis=0)
    high, low = split(spun)
    turned_back = (
        matmul(line_ref[...], high, (1, 1))
        + matmul(line_ref[...], low, (1, 1))
        + matmul(line_low[...], high, (1, 1))
    )
    back[...] = turned_back.reshape(back.shape)
    tall = GROUP * CHUNK // LANES
    base = 1 + groups

    def part(ref, g):
        return ref.at[:, pl.ds(pl.multiple_of(g * tall, tall), tall)]

    def up_copy(g):
        return copy(part(fields_ref, g), part(down, g), 1 + g, me + 1)

    def down_copy(g):
        return copy(part(fields_ref, g), part(up, g), base + 1 + g, me - 1)

    shape = perm_here.shape
    last = shape[0] - 1
    lane = lax.broadcasted_iota(jnp.int32, shape, 1)
    line = lax.broadcasted_iota(jnp.int32, shape, 0)

    def ahead_y(x):
        a = pltpu.roll(x, NZ, 1)
        return jnp.where(lane < NZ, a, pltpu.roll(a, last, 0))

    def behind_y(x):
        a = pltpu.roll(x, NZ, 1)
        return jnp.where(lane < NZ, pltpu.roll(a, 1, 0), a)

    def ahead_z(x):
        return pltpu.roll(x, LANES - 1, 1)

    def conduct():
        @pl.when(has_up)
        def _():
            to_up.start()

        @pl.when(has_down)
        def _():
            to_down.start()

        k = perm_here[...]
        inside = (line < last) | (lane < NZ)
        cond[1] = jnp.where(inside, open_ref[1].astype(F32) * harmonic(k, ahead_y(k)), 0.0)
        cond[2] = jnp.where(
            lane % NZ < NZ - 1, open_ref[2].astype(F32) * harmonic(k, ahead_z(k)), 0.0
        )

    sent_back = exchange(n, me, back, landed, lambda d: d, lambda d: slot(d, n), send_b, recv_b, conduct)
    across = landed[...].reshape(HALF, 4 * width).T
    quarter = HALF // 2
    re, im = (
        jnp.concatenate(
            [
                across[(2 * h + k) * width : (2 * h + k + 1) * width, p * quarter : (p + 1) * quarter]
                for p in range(2)
                for h in range(2)
            ],
            axis=1,
        )
        for k in range(2)
    )
    for j in range(CHUNKS // 2):
        c, s = turn_ref[0, j : j + 1, :], turn_ref[1, j : j + 1, :]
        spun_re, spun_im = split(re * c - im * s), split(im * c + re * s)
        for h in range(2):
            at = h * HALF
            rows = slice(j * width, (j + 1) * width)
            for k in range(2):
                turned[k, rows, 2 * at : 2 * at + HALF] = spun_re[k][:, at : at + HALF]
                turned[k, rows, 2 * at + HALF : 2 * at + KYZ] = spun_im[k][:, at : at + HALF]
    tile = 2 * LANES
    hid = in_ref.shape[1]
    tall_rows, tall_hid, pairs = GROUP * width, GROUP * hid, groups // 2
    for g in range(pairs):
        low = slice(g * tall_rows, (g + 1) * tall_rows)
        high = slice((g + pairs) * tall_rows, (g + pairs + 1) * tall_rows)
        for at in range(0, CHUNK, tile):
            cols = slice(at, at + tile)
            even, odd = (
                matmul(turned[0, low, side], table_ref[side, cols], (1, 0))
                + matmul(turned[1, low, side], table_ref[side, cols], (1, 0))
                + matmul(turned[0, low, side], fine_ref[side, cols], (1, 0))
                for side in (slice(0, KYZ), slice(KYZ, 2 * KYZ))
            )
            lifted[:tall_rows, cols] = gelu_twice(even + odd + skip[low, cols])
            lifted[tall_rows:, cols] = gelu_twice(even - odd + skip[high, cols])
        for k in range(2):
            at_g = g + k * pairs
            for at in range(0, CHUNK, tile):
                cols = slice(at, at + tile)
                hidden[k * tall_hid : (k + 1) * tall_hid, cols] = gelu_twice(
                    matmul(wide_in[...], lifted[k * tall_rows : (k + 1) * tall_rows, cols], (1, 0))
                )
            decoded = matmul(folded[...], hidden[k * tall_hid : (k + 1) * tall_hid, :], (1, 0))
            pressure = decoded[:GROUP] + decoded[GROUP : 2 * GROUP]
            saturation = jax.nn.sigmoid(decoded[2 * GROUP : 3 * GROUP] + decoded[3 * GROUP :])
            for r in range(CHUNK // LANES):
                where = pl.ds(at_g * tall + r, GROUP, stride=CHUNK // LANES)
                lanes = slice(r * LANES, (r + 1) * LANES)
                fields_ref[0, where, :] = pressure[:, lanes]
                fields_ref[1, where, :] = saturation[:, lanes]

            @pl.when(has_up)
            def _(at_g=at_g):
                up_copy(at_g).start()

            @pl.when(has_down)
            def _(at_g=at_g):
                down_copy(at_g).start()

    pressure, mobility = fields_ref[0], mobility_of(fields_ref[1])
    mob[...] = mobility
    flux = flux_of(cond[1], pressure, mobility, ahead_y(pressure), ahead_y(mobility))
    total = flux - behind_y(flux)
    flux = flux_of(cond[2], pressure, mobility, ahead_z(pressure), ahead_z(mobility))
    out_ref[...] = total + (flux - pltpu.roll(flux, 1, 1))
    @pl.when(has_up)
    def _():
        copy(perm_up, perm_up, base, me + 1).wait_recv()
        cond[0] = harmonic(gate[...], perm_up[...])

    @pl.when(has_down)
    def _():
        copy(gate_down, gate_down, 0, me - 1).wait_recv()
        cond[3] = harmonic(gate_down[...], perm_here[...])

    @pl.when(has_up)
    def _():
        for g in range(groups):
            copy(part(up, g), part(up, g), base + 1 + g, me + 1).wait_recv()
        out_ref[...] += flux_of(cond[0], fields_ref[0], mob[...], up[0], mobility_of(up[1]))

    @pl.when(has_down)
    def _():
        for g in range(groups):
            copy(part(down, g), part(down, g), 1 + g, me - 1).wait_recv()
        out_ref[...] -= flux_of(cond[3], down[0], mobility_of(down[1]), fields_ref[0], mob[...])

    @pl.when(has_up)
    def _():
        for c in [to_up] + [up_copy(g) for g in range(groups)]:
            c.wait_send()

    @pl.when(has_down)
    def _():
        for c in [to_down] + [down_copy(g) for g in range(groups)]:
            c.wait_send()

    sent.wait()
    sent_back.wait()


def mobility_of(s):
    return s * s / (s * s + 0.5 * (1.0 - s) * (1.0 - s))


def harmonic(a, b):
    return a * b / (a + b)


def flux_of(half, p, m, pn, mn):
    return half * (m + mn) * (p - pn)


def deliver_kernel(fields_ref, residual_ref, fields_out, residual_out, gone):
    stores = [
        pltpu.make_async_copy(src, dst, gone.at[k])
        for k, (src, dst) in enumerate([(fields_ref, fields_out), (residual_ref, residual_out)])
    ]
    for store in stores:
        store.start()
    for store in stores:
        store.wait()


def body(
    features,
    block_scale,
    spec_weight,
    bypass_weight,
    mlp_in,
    mlp_out,
    decode_weight,
    zone_ids,
    face_open,
    perm_table,
):
    width, rows, cells = features.shape
    n = lax.axis_size("gx")
    per = KYZ // n
    own = per * KX
    tall = cells // LANES
    zones = zone_ids.reshape(tall, LANES)
    opened = face_open.reshape(3, tall, LANES)
    flat = features.reshape(width, cells)
    order = line_order(n)
    table, turns, line = plane_table(order), chunk_turns(order), line_table(rows * n, per // 2)
    hid = mlp_in.shape[0]
    shape = (n, per // 2, 4 * width)
    block = pltpu.VMEM(shape, F32)
    sems = pltpu.SemaphoreType.DMA
    norm = 1.0 / (rows * n * NY * NZ)
    sources = (
        flat, block_scale.T, table[0], turns, *line, spec_weight,
        bypass_weight, mlp_in.T, mlp_out, decode_weight, zones, opened, perm_table, table[1],
    )
    plane = pltpu.VMEM((tall, LANES), F32)
    near = pltpu.VMEM((2, tall, LANES), F32)
    groups = CHUNKS // GROUP
    links = pltpu.SemaphoreType.DMA((2 + 2 * groups,))
    fields, residual = pl.pallas_call(
        lambda *refs: mode_kernel(n, norm, *refs),
        out_shape=(
            pltpu.VMEM((2, tall, LANES), F32),
            pltpu.VMEM((tall, LANES), F32),
        ),
        in_specs=[pl.BlockSpec(memory_space=pltpu.HBM)] * len(sources),
        out_specs=(VMEM, VMEM),
        scratch_shapes=[
            (pltpu.SMEM if source is perm_table else pltpu.VMEM)(source.shape, source.dtype)
            for source in sources
        ]
        + [
            pltpu.VMEM((CHUNKS * width, CHUNK), BF16),
            pltpu.VMEM((2, CHUNKS // 2 * width, 2 * KYZ), BF16),
            pltpu.VMEM((2 * GROUP * width, CHUNK), BF16),
            pltpu.VMEM((2 * GROUP * hid, CHUNK), BF16),
            pltpu.VMEM((CHUNKS * width, CHUNK), F32),
            pltpu.VMEM((4 * GROUP, GROUP * hid), BF16),
            pltpu.VMEM((GROUP * hid, GROUP * width), BF16),
            pltpu.VMEM((GROUP * width, GROUP * width), BF16),
            near,
            near,
            plane,
            plane,
            plane,
            plane,
            pltpu.VMEM((4, tall, LANES), F32),
            plane,
            links,
            links,
            block,
            block,
            pltpu.VMEM((2 * width, own), F32),
            block,
            block,
            pltpu.SemaphoreType.DMA((len(sources) + groups,)),
            sems,
            sems,
            sems,
            sems,
        ],
        compiler_params=pltpu.CompilerParams(
            vmem_limit_bytes=60 << 20, collective_id=0, has_side_effects=True
        ),
        name="layer",
    )(*(pltpu.with_memory_space_constraint(x, pltpu.HBM) for x in sources))
    anywhere = pl.BlockSpec(memory_space=pl.ANY)
    fields, residual = pl.pallas_call(
        deliver_kernel,
        out_shape=(
            jax.ShapeDtypeStruct((2, tall, LANES), F32),
            jax.ShapeDtypeStruct((tall, LANES), F32),
        ),
        in_specs=[VMEM, VMEM],
        out_specs=(anywhere, anywhere),
        scratch_shapes=[pltpu.SemaphoreType.DMA((2,))],
        name="deliver",
    )(*(pltpu.with_memory_space_constraint(x, pltpu.VMEM) for x in (fields, residual)))
    return fields.reshape(2, rows, cells), residual.reshape(rows, cells)


def solution(mesh):
    in_specs = (
        P(None, ("groups", "gx"), None),
        P(None, ("groups", "gx")),
        P(None, None, None, "gx"),
        P(),
        P(),
        P(),
        P(),
        P(("groups", "gx"), None),
        P(None, ("groups", "gx"), None),
        P(),
    )
    out_specs = (P(None, ("groups", "gx"), None), P(("groups", "gx"), None))
    return jax.shard_map(body, mesh=mesh, in_specs=in_specs, out_specs=out_specs, check_vma=False)
```

```python
import math

import jax
import jax.numpy as jnp
import numpy as np
from jax import lax
from jax.experimental import pallas as pl
from jax.experimental.pallas import tpu as pltpu
from jax.sharding import PartitionSpec as P

NY = 512
NZ = 64
KX = 32
KY = 32
KZ = 8
ZONES = 8
YC = 16
LANES = 128
KYZ = KY * KZ
HALF = KYZ // 2
CHUNK = YC * NZ
CHUNKS = NY // YC
GROUP = 8
F32 = jnp.float32
BF16 = jnp.bfloat16
VMEM = pl.BlockSpec(memory_space=pltpu.VMEM)


def signed(count):
    steps = np.arange(count)
    return np.where(steps < count // 2, steps, steps - count)


def pair(table):
    high = table.astype(BF16)
    low = (table - high.astype(np.float64)).astype(BF16)
    return jnp.asarray(high), jnp.asarray(low)


def line_order(n):
    per, share = KYZ // n, KZ * n // KYZ
    parity, half, spot, i = np.indices((2, 2, n // 2, per // 2))
    device = (2 * (spot // share) + parity) * share + spot % share
    return (device * per + half * (per // 2) + i).reshape(-1)


def plane_table(order):
    ky, kz = signed(KY)[order // KZ][:, None], (order % KZ)[:, None]
    yy = np.repeat(np.arange(YC), NZ)[None]
    zz = np.tile(np.arange(NZ), YC)[None]
    angle = 2.0 * math.pi * ((ky * yy / NY + kz * zz / NZ) % 1.0)
    parts = [part[at : at + HALF] for at in (0, HALF) for part in (np.cos(angle), -np.sin(angle))]
    return pair(np.concatenate(parts))


def chunk_turns(order):
    ky = signed(KY)[order // KZ][None]
    angle = 2.0 * math.pi * ((ky * (YC * np.arange(CHUNKS))[:, None] / NY) % 1.0)
    return jnp.asarray(np.stack([np.cos(angle), np.sin(angle)]).astype(np.float32))


def line_table(total_x, lines):
    angle = 2.0 * math.pi * ((signed(KX)[None] * np.arange(total_x)[:, None] / total_x) % 1.0)
    same = np.eye(lines)
    parts = [
        np.einsum("xk,lm->xlmk", part, same).reshape(total_x * lines, lines * KX)
        for part in (np.cos(angle), np.sin(angle))
    ]
    return pair(np.concatenate(parts, axis=1))


def gelu_twice(x):
    x = x.astype(BF16)
    return x + x * jnp.tanh(x * (BF16(0.7978845608028654) + BF16(0.035677408136300125) * (x * x)))


def matmul(a, b, dims):
    return lax.dot_general(a, b, ((dims[:1], dims[1:]), ((), ())), preferred_element_type=F32)


def column(row):
    count = row.shape[1]
    shape = (count, count)
    same = lax.broadcasted_iota(jnp.int32, shape, 0) == lax.broadcasted_iota(jnp.int32, shape, 1)
    return jnp.sum(jnp.where(same, row, 0.0), axis=1, keepdims=True)


def scaled(cells, scale):
    return (cells.astype(F32) * scale).astype(BF16)


def split(x):
    high = x.astype(BF16)
    return high, (x - high.astype(F32)).astype(BF16)


def fine(a, table, dims):
    high, low = split(a)
    return (
        matmul(high, table[0], dims) + matmul(low, table[0], dims) + matmul(high, table[1], dims)
    )


def forward(f_ref, scale, table_ref, turn_ref, held, ready):
    width = f_ref.shape[0]
    real = [jnp.zeros((width, HALF), F32)] * 2
    imag = [jnp.zeros((width, HALF), F32)] * 2
    step = 2 * GROUP
    for first in range(0, CHUNKS, step):
        for g in range(first // GROUP, (first + step) // GROUP):
            ready(g)
        for j in range(first, first + step):
            held[j * width : (j + 1) * width, :] = scaled(
                f_ref[:, j * CHUNK : (j + 1) * CHUNK], scale
            )
        part = matmul(held[first * width : (first + step) * width, :], table_ref[...], (1, 1))
        for j in range(first, first + step):
            rows = part[(j - first) * width : (j - first + 1) * width]
            for h in range(2):
                at = h * HALF
                re, im = rows[:, 2 * at : 2 * at + HALF], rows[:, 2 * at + HALF : 2 * at + KYZ]
                c, s = (turn_ref[k, j : j + 1, at : at + HALF] for k in range(2))
                real[h] = real[h] + re * c + im * s
                imag[h] = imag[h] + im * c - re * s
    both = [jnp.concatenate([x, y], axis=0) for x, y in zip(real, imag)]
    quarter = HALF // 2
    tall = [jnp.concatenate([x[:, :quarter], x[:, quarter:]], axis=0) for x in both]
    return jnp.concatenate(tall, axis=1).T


def slot(device, n):
    share = KZ * n // KYZ
    if share == 1:
        return lax.rem(device, 2) * (KY // 2) + lax.div(device, 2)
    ky = lax.div(device, share)
    return (lax.rem(ky, 2) * (KY // 2) + lax.div(ky, 2)) * share + lax.rem(device, share)


def exchange(n, me, src, dst, place, spot, send_sem, recv_sem, meanwhile=None):
    def copy(d):
        peer = lax.rem(me + d, n)
        return pltpu.make_async_remote_copy(
            src_ref=src.at[place(peer)],
            dst_ref=dst.at[spot(me)],
            send_sem=send_sem,
            recv_sem=recv_sem,
            device_id={"gx": peer},
            device_id_type=pl.DeviceIdType.MESH,
        )

    def start(d, carry):
        copy(d).start()
        return carry

    lax.fori_loop(1, n, start, 0)
    dst[spot(me)] = src[place(me)]
    if meanwhile is not None:
        meanwhile()
    landing = dst.at[pl.ds(0, n - 1)]
    pltpu.make_async_copy(landing, landing, recv_sem).wait()
    return pltpu.make_async_copy(landing, landing, send_sem)


def one_hot(rows, cols, on_row, on_col):
    row = on_row(lax.broadcasted_iota(jnp.int32, (rows, cols), 0))
    col = on_col(lax.broadcasted_iota(jnp.int32, (rows, cols), 1))
    return jnp.where(row == col, 1.0, 0.0)


def block_diagonal(weight, rows, cols):
    tall = matmul(
        one_hot(GROUP * rows, rows, lambda r: r % rows, lambda c: c).astype(BF16), weight, (1, 0)
    ).astype(BF16)
    full = matmul(
        tall, one_hot(cols, GROUP * cols, lambda r: r, lambda c: c % cols).astype(BF16), (1, 0)
    )
    mask = one_hot(GROUP * rows, GROUP * cols, lambda r: r // rows, lambda c: c // cols)
    return (full * mask).astype(BF16)


def mode_kernel(
    n, norm, f_hbm, scale_hbm, table_hbm, turn_hbm, line_hbm, line_low_hbm, w_hbm,
    bypass_hbm, in_hbm, outw_hbm, dec_hbm, zone_hbm, open_hbm, perm_hbm, fine_hbm, fields_ref, out_ref,
    f_ref, scale_ref, table_ref, turn_ref, line_ref, line_low, w_ref,
    bypass_ref, in_ref, outw_ref, dec_ref, zone_ref, open_ref, perm_ref, fine_ref,
    held, turned, lifted, hidden, skip, folded, wide_in, wide_by, up, down,
    perm_here, gate, perm_up, gate_down, cond, mob, send, recv,
    a_ref, lines, modes, back, landed, load_sem, send_a, recv_a, send_b, recv_b,
):
    me = lax.axis_index("gx")
    barrier = pltpu.get_barrier_semaphore()

    def greet(d, carry):
        pl.semaphore_signal(
            barrier, inc=1, device_id={"gx": lax.rem(me + d, n)},
            device_id_type=pl.DeviceIdType.MESH,
        )
        return carry

    lax.fori_loop(1, n, greet, 0)
    groups = CHUNKS // GROUP
    span = GROUP * CHUNK
    pieces = [
        (f_hbm.at[:, g * span : (g + 1) * span], f_ref.at[:, g * span : (g + 1) * span])
        for g in range(groups)
    ]
    wanted = [(table_hbm, table_ref), (scale_hbm, scale_ref), (turn_hbm, turn_ref)]
    wanted += pieces + [(line_hbm, line_ref), (line_low_hbm, line_low), (w_hbm, w_ref)]
    wanted += [(bypass_hbm, bypass_ref), (in_hbm, in_ref), (outw_hbm, outw_ref)]
    wanted += [(dec_hbm, dec_ref), (zone_hbm, zone_ref), (open_hbm, open_ref)]
    wanted += [(perm_hbm, perm_ref), (fine_hbm, fine_ref)]
    loads = [
        pltpu.make_async_copy(src, dst, load_sem.at[k]) for k, (src, dst) in enumerate(wanted)
    ]
    for load in loads:
        load.start()
    for load in loads[:3]:
        load.wait()
    scale = column(scale_ref[...])
    seen = forward(
        f_ref, scale, table_ref, turn_ref, held, lambda g: loads[3 + g].wait()
    )
    a_ref[...] = seen.reshape(a_ref.shape)
    pl.semaphore_wait(barrier, n - 1)

    def lookup(zones):
        total = jnp.zeros(zones.shape, F32)
        for zone in range(ZONES):
            total = jnp.where(zones == zone, perm_ref[zone], total)
        return total

    def weights():
        for load in loads[3 + groups :]:
            load.wait()
        perm_here[...] = lookup(zone_ref[...])
        gate[...] = open_ref[0].astype(F32) * perm_here[...]
        width, hid = in_ref.shape
        fold = jnp.dot(dec_ref[...], outw_ref[...], preferred_element_type=F32) * 0.5
        high = fold.astype(BF16).astype(F32)
        low = fold - high
        row = lax.broadcasted_iota(jnp.int32, (GROUP, hid), 0)
        for r in range(GROUP):
            rows = [
                jnp.where(row == r, part[k : k + 1, :], 0.0)
                for k in range(2)
                for part in (high, low)
            ]
            folded[:, r * hid : (r + 1) * hid] = jnp.concatenate(rows, axis=0).astype(BF16)
        wide_by[...] = block_diagonal(bypass_ref[...], width, width)
        wide_in[...] = block_diagonal(in_ref[...].T, hid, width) * BF16(0.5)
        tall_rows = GROUP * width

        def bypass(g, carry):
            rows = pl.ds(pl.multiple_of(g * tall_rows, tall_rows), tall_rows)
            skip[rows, :] = matmul(wide_by[...], held[rows, :], (1, 0))
            return carry

        lax.fori_loop(0, groups, bypass, 0)

    sent = exchange(n, me, a_ref, lines, lambda d: slot(d, n), lambda d: d, send_a, recv_a, weights)
    has_up, has_down = me < n - 1, me > 0

    def copy(src, dst, at, peer):
        return pltpu.make_async_remote_copy(
            src_ref=src, dst_ref=dst, send_sem=send.at[at], recv_sem=recv.at[at],
            device_id={"gx": peer}, device_id_type=pl.DeviceIdType.MESH,
        )

    to_up = copy(gate, gate_down, 0, me + 1)
    to_down = copy(perm_here, perm_up, 1 + groups, me - 1)

    count, few, wide = lines.shape
    both = wide // 2
    width, own = both // 2, few * KX
    spread = fine(lines[...].reshape(count * few, wide), (line_ref[...], line_low[...]), (0, 0))
    for h in range(2):
        re, im = (spread[h * both + k * width : h * both + (k + 1) * width] for k in range(2))
        cols = slice(h * own, (h + 1) * own)
        modes[:width, cols] = re[:, :own] + im[:, own:]
        modes[width:, cols] = im[:, :own] - re[:, own:]

    def mix(i, carry):
        real, imag = carry
        re, im = modes[pl.ds(i, 1), :], modes[pl.ds(width + i, 1), :]
        wr, wi = w_ref[0, i].astype(F32), w_ref[1, i].astype(F32)
        return real + (re * wr - im * wi), imag + (re * wi + im * wr)

    zero = jnp.zeros((width, 2 * own), F32)
    real, imag = lax.fori_loop(0, width, mix, (zero, zero), unroll=4)
    line = me * 2 * few + lax.broadcasted_iota(jnp.int32, (1, 2 * own), 1) // KX
    weight = jnp.where(line % KZ == 0, norm, 2.0 * norm)
    real, imag = real * weight, imag * weight
    rows = []
    for h in range(2):
        re, im = (x[:, h * own : (h + 1) * own] for x in (real, imag))
        rows += [jnp.concatenate([re, -im], axis=1), jnp.concatenate([im, re], axis=1)]
    spun = jnp.concatenate(rows, axis=0)
    high, low = split(spun)
    turned_back = (
        matmul(line_ref[...], high, (1, 1))
        + matmul(line_ref[...], low, (1, 1))
        + matmul(line_low[...], high, (1, 1))
    )
    back[...] = turned_back.reshape(back.shape)
    tall = GROUP * CHUNK // LANES
    base = 1 + groups

    def part(ref, g):
        return ref.at[:, pl.ds(pl.multiple_of(g * tall, tall), tall)]

    def up_copy(g):
        return copy(part(fields_ref, g), part(down, g), 1, me + 1)

    def down_copy(g):
        return copy(part(fields_ref, g), part(up, g), base + 1, me - 1)

    shape = perm_here.shape
    last = shape[0] - 1
    lane = lax.broadcasted_iota(jnp.int32, shape, 1)
    line = lax.broadcasted_iota(jnp.int32, shape, 0)

    def ahead_y(x):
        a = pltpu.roll(x, NZ, 1)
        return jnp.where(lane < NZ, a, pltpu.roll(a, last, 0))

    def behind_y(x):
        a = pltpu.roll(x, NZ, 1)
        return jnp.where(lane < NZ, pltpu.roll(a, 1, 0), a)

    def ahead_z(x):
        return pltpu.roll(x, LANES - 1, 1)

    def conduct():
        @pl.when(has_up)
        def _():
            to_up.start()

        @pl.when(has_down)
        def _():
            to_down.start()

        k = perm_here[...]
        inside = (line < last) | (lane < NZ)
        cond[1] = jnp.where(inside, open_ref[1].astype(F32) * harmonic(k, ahead_y(k)), 0.0)
        cond[2] = jnp.where(
            lane % NZ < NZ - 1, open_ref[2].astype(F32) * harmonic(k, ahead_z(k)), 0.0
        )

    sent_back = exchange(n, me, back, landed, lambda d: d, lambda d: slot(d, n), send_b, recv_b, conduct)
    across = landed[...].reshape(HALF, 4 * width).T
    quarter = HALF // 2
    re, im = (
        jnp.concatenate(
            [
                across[(2 * h + k) * width : (2 * h + k + 1) * width, p * quarter : (p + 1) * quarter]
                for p in range(2)
                for h in range(2)
            ],
            axis=1,
        )
        for k in range(2)
    )
    for j in range(CHUNKS // 2):
        c, s = turn_ref[0, j : j + 1, :], turn_ref[1, j : j + 1, :]
        spun_re, spun_im = split(re * c - im * s), split(im * c + re * s)
        for h in range(2):
            at = h * HALF
            rows = slice(j * width, (j + 1) * width)
            for k in range(2):
                turned[k, rows, 2 * at : 2 * at + HALF] = spun_re[k][:, at : at + HALF]
                turned[k, rows, 2 * at + HALF : 2 * at + KYZ] = spun_im[k][:, at : at + HALF]
    tile = 2 * LANES
    hid = in_ref.shape[1]
    tall_rows, tall_hid, pairs = GROUP * width, GROUP * hid, groups // 2
    for g in range(pairs):
        low = slice(g * tall_rows, (g + 1) * tall_rows)
        high = slice((g + pairs) * tall_rows, (g + pairs + 1) * tall_rows)
        for at in range(0, CHUNK, tile):
            cols = slice(at, at + tile)
            even, odd = (
                matmul(turned[0, low, side], table_ref[side, cols], (1, 0))
                + matmul(turned[1, low, side], table_ref[side, cols], (1, 0))
                + matmul(turned[0, low, side], fine_ref[side, cols], (1, 0))
                for side in (slice(0, KYZ), slice(KYZ, 2 * KYZ))
            )
            lifted[:tall_rows, cols] = gelu_twice(even + odd + skip[low, cols])
            lifted[tall_rows:, cols] = gelu_twice(even - odd + skip[high, cols])
        for k in range(2):
            at_g = g + k * pairs
            for at in range(0, CHUNK, tile):
                cols = slice(at, at + tile)
                hidden[k * tall_hid : (k + 1) * tall_hid, cols] = gelu_twice(
                    matmul(wide_in[...], lifted[k * tall_rows : (k + 1) * tall_rows, cols], (1, 0))
                )
            decoded = matmul(folded[...], hidden[k * tall_hid : (k + 1) * tall_hid, :], (1, 0))
            pressure = decoded[:GROUP] + decoded[GROUP : 2 * GROUP]
            saturation = jax.nn.sigmoid(decoded[2 * GROUP : 3 * GROUP] + decoded[3 * GROUP :])
            for r in range(CHUNK // LANES):
                where = pl.ds(at_g * tall + r, GROUP, stride=CHUNK // LANES)
                lanes = slice(r * LANES, (r + 1) * LANES)
                fields_ref[0, where, :] = pressure[:, lanes]
                fields_ref[1, where, :] = saturation[:, lanes]

            @pl.when(has_up)
            def _(at_g=at_g):
                up_copy(at_g).start()

            @pl.when(has_down)
            def _(at_g=at_g):
                down_copy(at_g).start()

    pressure, mobility = fields_ref[0], mobility_of(fields_ref[1])
    mob[...] = mobility
    flux = flux_of(cond[1], pressure, mobility, ahead_y(pressure), ahead_y(mobility))
    total = flux - behind_y(flux)
    flux = flux_of(cond[2], pressure, mobility, ahead_z(pressure), ahead_z(mobility))
    out_ref[...] = total + (flux - pltpu.roll(flux, 1, 1))
    @pl.when(has_up)
    def _():
        copy(perm_up, perm_up, base, me + 1).wait_recv()
        cond[0] = harmonic(gate[...], perm_up[...])

    @pl.when(has_down)
    def _():
        copy(gate_down, gate_down, 0, me - 1).wait_recv()
        cond[3] = harmonic(gate_down[...], perm_here[...])

    @pl.when(has_up)
    def _():
        copy(up, up, base + 1, me + 1).wait_recv()
        out_ref[...] += flux_of(cond[0], fields_ref[0], mob[...], up[0], mobility_of(up[1]))

    @pl.when(has_down)
    def _():
        copy(down, down, 1, me - 1).wait_recv()
        out_ref[...] -= flux_of(cond[3], down[0], mobility_of(down[1]), fields_ref[0], mob[...])

    @pl.when(has_up)
    def _():
        for c in [to_up, copy(fields_ref, down, 1, me + 1)]:
            c.wait_send()

    @pl.when(has_down)
    def _():
        for c in [to_down, copy(fields_ref, up, base + 1, me - 1)]:
            c.wait_send()

    sent.wait()
    sent_back.wait()


def mobility_of(s):
    return s * s / (s * s + 0.5 * (1.0 - s) * (1.0 - s))


def harmonic(a, b):
    return a * b / (a + b)


def flux_of(half, p, m, pn, mn):
    return half * (m + mn) * (p - pn)


def deliver_kernel(fields_ref, residual_ref, fields_out, residual_out, gone):
    stores = [
        pltpu.make_async_copy(src, dst, gone.at[k])
        for k, (src, dst) in enumerate([(fields_ref, fields_out), (residual_ref, residual_out)])
    ]
    for store in stores:
        store.start()
    for store in stores:
        store.wait()


def body(
    features,
    block_scale,
    spec_weight,
    bypass_weight,
    mlp_in,
    mlp_out,
    decode_weight,
    zone_ids,
    face_open,
    perm_table,
):
    width, rows, cells = features.shape
    n = lax.axis_size("gx")
    per = KYZ // n
    own = per * KX
    tall = cells // LANES
    zones = zone_ids.reshape(tall, LANES)
    opened = face_open.reshape(3, tall, LANES)
    flat = features.reshape(width, cells)
    order = line_order(n)
    table, turns, line = plane_table(order), chunk_turns(order), line_table(rows * n, per // 2)
    hid = mlp_in.shape[0]
    shape = (n, per // 2, 4 * width)
    block = pltpu.VMEM(shape, F32)
    sems = pltpu.SemaphoreType.DMA
    norm = 1.0 / (rows * n * NY * NZ)
    sources = (
        flat, block_scale.T, table[0], turns, *line, spec_weight,
        bypass_weight, mlp_in.T, mlp_out, decode_weight, zones, opened, perm_table, table[1],
    )
    plane = pltpu.VMEM((tall, LANES), F32)
    near = pltpu.VMEM((2, tall, LANES), F32)
    groups = CHUNKS // GROUP
    links = pltpu.SemaphoreType.DMA((2 + 2 * groups,))
    fields, residual = pl.pallas_call(
        lambda *refs: mode_kernel(n, norm, *refs),
        out_shape=(
            pltpu.VMEM((2, tall, LANES), F32),
            pltpu.VMEM((tall, LANES), F32),
        ),
        in_specs=[pl.BlockSpec(memory_space=pltpu.HBM)] * len(sources),
        out_specs=(VMEM, VMEM),
        scratch_shapes=[
            (pltpu.SMEM if source is perm_table else pltpu.VMEM)(source.shape, source.dtype)
            for source in sources
        ]
        + [
            pltpu.VMEM((CHUNKS * width, CHUNK), BF16),
            pltpu.VMEM((2, CHUNKS // 2 * width, 2 * KYZ), BF16),
            pltpu.VMEM((2 * GROUP * width, CHUNK), BF16),
            pltpu.VMEM((2 * GROUP * hid, CHUNK), BF16),
            pltpu.VMEM((CHUNKS * width, CHUNK), F32),
            pltpu.VMEM((4 * GROUP, GROUP * hid), BF16),
            pltpu.VMEM((GROUP * hid, GROUP * width), BF16),
            pltpu.VMEM((GROUP * width, GROUP * width), BF16),
            near,
            near,
            plane,
            plane,
            plane,
            plane,
            pltpu.VMEM((4, tall, LANES), F32),
            plane,
            links,
            links,
            block,
            block,
            pltpu.VMEM((2 * width, own), F32),
            block,
            block,
            pltpu.SemaphoreType.DMA((len(sources) + groups,)),
            sems,
            sems,
            sems,
            sems,
        ],
        compiler_params=pltpu.CompilerParams(
            vmem_limit_bytes=60 << 20, collective_id=0, has_side_effects=True
        ),
        name="layer",
    )(*(pltpu.with_memory_space_constraint(x, pltpu.HBM) for x in sources))
    anywhere = pl.BlockSpec(memory_space=pl.ANY)
    fields, residual = pl.pallas_call(
        deliver_kernel,
        out_shape=(
            jax.ShapeDtypeStruct((2, tall, LANES), F32),
            jax.ShapeDtypeStruct((tall, LANES), F32),
        ),
        in_specs=[VMEM, VMEM],
        out_specs=(anywhere, anywhere),
        scratch_shapes=[pltpu.SemaphoreType.DMA((2,))],
        name="deliver",
    )(*(pltpu.with_memory_space_constraint(x, pltpu.VMEM) for x in (fields, residual)))
    return fields.reshape(2, rows, cells), residual.reshape(rows, cells)


def solution(mesh):
    in_specs = (
        P(None, ("groups", "gx"), None),
        P(None, ("groups", "gx")),
        P(None, None, None, "gx"),
        P(),
        P(),
        P(),
        P(),
        P(("groups", "gx"), None),
        P(None, ("groups", "gx"), None),
        P(),
    )
    out_specs = (P(None, ("groups", "gx"), None), P(("groups", "gx"), None))
    return jax.shard_map(body, mesh=mesh, in_specs=in_specs, out_specs=out_specs, check_vma=False)
```
